1024 devices in a mesh: seq: 32 (over x, y_hi, core), chan: 32 (over z, y_lo).
Axes of the slice: x: 4, y: 8 (y_hi: 4, y_lo: 2; y = y_hi * 2 + y_lo), z: 16, core: 2. Of those that a mesh axis runs over, the one named last changes fastest.
Arguments:
- query_proj: bfloat16 [4096, 4096], P('chan', 'seq'), may hold values from -6 to 6
- key_proj: bfloat16 [4096, 4096], P('chan', 'seq'), may hold values from -6 to 6
- value_proj: bfloat16 [4096, 4096], P('chan', 'seq'), may hold values from -6 to 6
- cotangent: bfloat16 [4096, 4096], P('chan', 'seq'), may hold values from -6 to 6
- filter_taps: bfloat16 [128, 4096], P('seq'), may hold values from -6 to 6
Outputs:
- gated_out: bfloat16 [4096, 4096], P('chan', 'seq')
- query_grad: bfloat16 [4096, 4096], P('chan', 'seq')
- key_grad: bfloat16 [4096, 4096], P('chan', 'seq')
- value_grad: bfloat16 [4096, 4096], P('chan', 'seq')
- filter_grad: float32 [128, 4096], P('seq', 'chan')
The draws below stay inside these ranges and needn't reach their ends.
All inputs are finite; a program needn't handle non-finite values.
Results may differ from the reference program's by a relative error of at most 0.0057.
Values may be sent and summed in bfloat16 or wider, within the bound.
A program may use at most 32 MiB of HBM per device.

```python
import math
import jax
import jax.numpy as jnp
from jax import lax

D = 4096
LEN = 4096
NF = 128
N_CHAN = 32


def shard_levels(stream_key, dims, pieces, low, high):
    factor_of = 1.0
    for axis_at, parts in pieces:
        draws = jax.random.uniform(jax.random.fold_in(jax.random.fold_in(stream_key, 6), axis_at), (parts,), jnp.float32, low / len(pieces), high / len(pieces))
        factor_of = factor_of * jnp.repeat(jnp.exp(draws), dims[axis_at] // parts).reshape((-1,) + (1,) * (len(dims) - 1 - axis_at))
    return factor_of


def centred(rng, extent, scale, reach, pieces=(), kind=jnp.bfloat16):
    result = jax.random.normal(rng, extent, jnp.float32) * scale
    if len(pieces) > 0:
        result = shard_levels(rng, extent, pieces, -0.22, 0.18) * result
    return jnp.clip(result, min=-reach, max=reach).astype(kind)


def setup_inputs(seed: int = 0) -> dict:
    streams_of = jax.random.split(jax.random.key(seed), 6)
    return {
        "query_proj": centred(streams_of[0], (D, LEN), 1.0, 6.0, ((0, 32), (1, 32))),
        "key_proj": centred(streams_of[1], (D, LEN), 1.0, 6.0, ((0, 32), (1, 32))),
        "value_proj": centred(streams_of[2], (D, LEN), 1.0, 6.0, ((0, 32), (1, 32))),
        "cotangent": centred(streams_of[3], (D, LEN), 1.0, 6.0, ((0, 32), (1, 32))),
        "filter_taps": centred(streams_of[4], (NF, LEN), 1.0, 6.0, ((0, 32),)),
    }


def reference(query_proj, key_proj, value_proj, cotangent, filter_taps):
    scale = 1.0 / math.sqrt(LEN)
    taps = filter_taps.astype(jnp.float32) * scale
    filt_spec = jnp.fft.fft(taps, n=2 * LEN, axis=1)

    def block(index):
        start = (index * NF).astype(jnp.int32)
        query = lax.dynamic_slice_in_dim(query_proj, start, NF, 0).astype(jnp.float32)
        keyset = lax.dynamic_slice_in_dim(key_proj, start, NF, 0).astype(jnp.float32)
        values = lax.dynamic_slice_in_dim(value_proj, start, NF, 0).astype(jnp.float32)
        upstream = lax.dynamic_slice_in_dim(cotangent, start, NF, 0).astype(jnp.float32)
        mixed = (keyset * values).astype(jnp.bfloat16)
        pulled = (upstream * query).astype(jnp.bfloat16)
        mix_spec = jnp.fft.fft(mixed.astype(jnp.float32), n=2 * LEN, axis=1)
        pull_spec = jnp.fft.fft(pulled.astype(jnp.float32), n=2 * LEN, axis=1)
        conv = jnp.fft.ifft(mix_spec * filt_spec, axis=1).real[:, :LEN].astype(jnp.bfloat16)
        back = jnp.fft.ifft(pull_spec * jnp.conj(filt_spec), axis=1).real[:, :LEN].astype(jnp.bfloat16)
        lag = jnp.fft.ifft(pull_spec * jnp.conj(mix_spec), axis=1).real[:, :LEN] * scale
        conv_wide = conv.astype(jnp.float32)
        back_wide = back.astype(jnp.float32)
        gated = (query * conv_wide).astype(jnp.bfloat16)
        qgrad = (upstream * conv_wide).astype(jnp.bfloat16)
        kgrad = (back_wide * values).astype(jnp.bfloat16)
        vgrad = (back_wide * keyset).astype(jnp.bfloat16)
        return (gated, qgrad, kgrad, vgrad, lag.astype(jnp.float32))
    gated, qgrad, kgrad, vgrad, lags = lax.map(block, jnp.arange(N_CHAN, dtype=jnp.int32))
    filter_grad = lax.optimization_barrier(jnp.sum(lags, axis=0))
    return (gated.reshape(D, LEN), qgrad.reshape(D, LEN), kgrad.reshape(D, LEN), vgrad.reshape(D, LEN), filter_grad)
```

```python
import functools
import math

import jax
import jax.numpy as jnp
from jax import lax
from jax.experimental import pallas as pl
from jax.experimental.pallas import tpu as pltpu
from jax.sharding import PartitionSpec as P

MESH = pl.DeviceIdType.MESH
F32 = jnp.float32
BF16 = jnp.bfloat16
W = 128
CH = 4


def flip_matrix():
    row = lax.broadcasted_iota(jnp.int32, (W, W), 0)
    col = lax.broadcasted_iota(jnp.int32, (W, W), 1)
    return jnp.where(row + col == W - 1, 1.0, 0.0).astype(BF16)


def dot(left, right):
    return jnp.dot(left, right, preferred_element_type=F32)


def write_toeplitz(blocks, row_of, out_ref):
    row = lax.broadcasted_iota(jnp.int32, (W, W), 0)
    col = lax.broadcasted_iota(jnp.int32, (W, W), 1)
    lower = row >= col
    before = jnp.zeros((W, W), F32)
    for k in range(blocks):
        turned = pltpu.roll(
            jnp.broadcast_to(row_of(k), (W, W)), 1, 1, stride=1, stride_axis=0
        )
        out_ref[W * k : W * (k + 1), :] = jnp.where(lower, turned, before).astype(BF16)
        before = turned


def kernel(
    n, scale,
    q_hbm, k_hbm, v_hbm, g_hbm, taps_hbm,
    gated_ref, qgrad_ref, kgrad_ref, vgrad_ref, fgrad_ref,
    q, k, v, g, taps, in_sem,
    send1, recv1, send2, recv2, send3, recv3, sems,
    tap_rows, tap_flip, wide1, flip1, pad_p, pad_x, filt_toe, x_toe, lhs, wide2,
):
    me_seq = lax.axis_index("seq")
    me_chan = lax.axis_index("chan")

    loads = [
        pltpu.make_async_copy(src, dst, in_sem.at[i])
        for i, (src, dst) in enumerate(
            ((k_hbm, k), (v_hbm, v), (g_hbm, g), (q_hbm, q), (taps_hbm, taps))
        )
    ]
    for load in loads:
        load.start()

    barrier = pltpu.get_barrier_semaphore()

    def greet(i, carry):
        pl.semaphore_signal(
            barrier, inc=1, device_id={"seq": lax.rem(me_seq + i, n)}, device_id_type=MESH
        )
        pl.semaphore_signal(
            barrier, inc=1, device_id={"chan": lax.rem(me_chan + i, n)}, device_id_type=MESH
        )
        return carry

    lax.fori_loop(1, n, greet, 0)

    half = lax.broadcasted_iota(jnp.int32, (CH * n // 8, 8, W), 1) < CH

    def swap(x):
        return pltpu.roll(x, CH, 1)

    for load in loads[:4]:
        load.wait()
    tiles = (CH * n // 8, 8, W)
    mixed = (k[...].astype(F32) * v[...].astype(F32)).reshape(tiles)
    pulled = (g[...].astype(F32) * q[...].astype(F32)).reshape(tiles)
    pair = jnp.stack(
        [jnp.where(half, mixed, swap(pulled)), jnp.where(half, swap(mixed), pulled)], axis=1
    )
    send1[...] = pair.reshape(n, 8, W).astype(BF16)

    pl.semaphore_wait(barrier, 2 * (n - 1))

    def exchange(axis, me, send, recv, at):
        def step(i, carry):
            to = lax.rem(me + i, n)
            pltpu.make_async_remote_copy(
                src_ref=send.at[to], dst_ref=recv.at[me],
                send_sem=sems.at[at], recv_sem=sems.at[at + 1],
                device_id={axis: to}, device_id_type=MESH,
            ).start()
            return carry

        lax.fori_loop(1, n, step, 0)
        recv[me] = send[me]

    def all_of(axis, me, send, recv, at):
        return pltpu.make_async_remote_copy(
            src_ref=send.at[pl.ds(0, n - 1)], dst_ref=recv.at[pl.ds(0, n - 1)],
            send_sem=sems.at[at], recv_sem=sems.at[at + 1],
            device_id={axis: lax.rem(me + 1, n)}, device_id_type=MESH,
        )

    exchange("seq", me_seq, send1, recv1, 0)

    flip = flip_matrix()
    loads[4].wait()
    tap_values = taps[...].astype(F32)
    for b in range(n):
        tap_rows[CH * b : CH * (b + 1), :] = tap_values[:, W * b : W * (b + 1)]
    tap_flip[...] = dot(tap_rows[...].astype(BF16), flip)

    def filter_matrix(c, carry):
        write_toeplitz(n, lambda b: tap_flip[pl.ds(CH * b + c, 1), :], filt_toe.at[c])
        return carry

    lax.fori_loop(0, CH, filter_matrix, 0)
    pad_p[...] = jnp.zeros_like(pad_p)
    pad_x[...] = jnp.zeros_like(pad_x)

    all_of("seq", me_seq, send1, recv1, 0).wait_recv()
    got = recv1[...].reshape(n * 8, W)
    wide1[...] = got.astype(F32)
    flip1[...] = dot(got, flip)

    def convolve(c, carry):
        pad_p[:n, :] = wide1[pl.ds(CH + c, n, stride=8), :]
        pad_x[n:, :] = flip1[pl.ds(c, n, stride=8), :]
        for b in range(n):
            lhs[c, :n, W * b : W * (b + 1)] = pad_p[b : b + n, :].astype(BF16)
            lhs[c, n:, W * b : W * (b + 1)] = pad_x[n - b : 2 * n - b, :].astype(BF16)
        both = dot(lhs[c], filt_toe[c]) * scale
        wide2[pl.ds(c, n, stride=8), :] = both[n:]
        wide2[pl.ds(CH + c, n, stride=8), :] = both[:n]
        return carry

    lax.fori_loop(0, CH, convolve, 0)
    send2[...] = wide2[...].reshape(n, 8, W).astype(BF16)
    exchange("seq", me_seq, send2, recv2, 2)

    def lags(c, carry):
        write_toeplitz(n, lambda b: flip1[pl.ds(8 * b + c, 1), :], x_toe)
        wide2[pl.ds(c, n, stride=8), :] = dot(lhs[c, :n, :], x_toe[...]) * scale
        return carry

    lax.fori_loop(0, CH, lags, 0)
    send3[...] = wide2[...].reshape(n, 8, W)[:, :CH, :]
    exchange("chan", me_chan, send3, recv3, 4)

    all_of("seq", me_seq, send2, recv2, 2).wait_recv()
    came = recv2[...].astype(F32).reshape(CH * n // 8, 2, 8, W)
    low, high = came[:, 0], came[:, 1]
    conv = jnp.where(half, low, swap(high)).reshape(CH * n, W)
    back = jnp.where(half, swap(low), high).reshape(CH * n, W)
    conv = dot(conv.astype(BF16), flip)
    gated_ref[...] = (q[...].astype(F32) * conv).astype(BF16)
    qgrad_ref[...] = (g[...].astype(F32) * conv).astype(BF16)
    kgrad_ref[...] = (back * v[...].astype(F32)).astype(BF16)
    vgrad_ref[...] = (back * k[...].astype(F32)).astype(BF16)

    all_of("chan", me_chan, send3, recv3, 4).wait_recv()
    fgrad_ref[...] = jnp.sum(recv3[...], axis=0)

    all_of("seq", me_seq, send1, recv1, 0).wait_send()
    all_of("seq", me_seq, send2, recv2, 2).wait_send()
    all_of("chan", me_chan, send3, recv3, 4).wait_send()


def on_device(n, query_proj, key_proj, value_proj, cotangent, filter_taps):
    rows = CH * n
    length = W * n
    vmem = pl.BlockSpec(memory_space=pltpu.VMEM)
    hbm = pl.BlockSpec(memory_space=pltpu.HBM)
    slab = jax.ShapeDtypeStruct((rows, W), BF16)
    return pl.pallas_call(
        functools.partial(kernel, n, 1.0 / math.sqrt(length)),
        out_shape=(slab, slab, slab, slab, jax.ShapeDtypeStruct((CH, W), F32)),
        in_specs=[hbm] * 5,
        out_specs=(vmem,) * 5,
        scratch_shapes=[pltpu.VMEM((rows, W), BF16)] * 4
        + [
            pltpu.VMEM((CH, length), BF16),
            pltpu.SemaphoreType.DMA((5,)),
            pltpu.VMEM((n, 8, W), BF16),
            pltpu.VMEM((n, 8, W), BF16),
            pltpu.VMEM((n, 8, W), BF16),
            pltpu.VMEM((n, 8, W), BF16),
            pltpu.VMEM((n, CH, W), F32),
            pltpu.VMEM((n, CH, W), F32),
            pltpu.SemaphoreType.DMA((6,)),
            pltpu.VMEM((rows, W), F32),
            pltpu.VMEM((rows, W), F32),
            pltpu.VMEM((8 * n, W), F32),
            pltpu.VMEM((8 * n, W), F32),
            pltpu.VMEM((2 * n, W), F32),
            pltpu.VMEM((2 * n, W), F32),
            pltpu.VMEM((CH, length, W), BF16),
            pltpu.VMEM((length, W), BF16),
            pltpu.VMEM((CH, 2 * n, length), BF16),
            pltpu.VMEM((8 * n, W), F32),
        ],
        compiler_params=pltpu.CompilerParams(
            collective_id=0, has_side_effects=True, vmem_limit_bytes=32 << 20
        ),
    )(*(pltpu.with_memory_space_constraint(x, pltpu.HBM) for x in (query_proj, key_proj, value_proj, cotangent, filter_taps)))


def solution(mesh):
    return jax.shard_map(
        functools.partial(on_device, mesh.shape["seq"]),
        mesh=mesh,
        in_specs=(
            P("chan", "seq"),
            P("chan", "seq"),
            P("chan", "seq"),
            P("chan", "seq"),
            P("seq", None),
        ),
        out_specs=(
            P("chan", "seq"),
            P("chan", "seq"),
            P("chan", "seq"),
            P("chan", "seq"),
            P("seq", "chan"),
        ),
        check_vma=False,
    )
```

```python
import functools
import math

import jax
import jax.numpy as jnp
from jax import lax
from jax.experimental import pallas as pl
from jax.experimental.pallas import tpu as pltpu
from jax.sharding import PartitionSpec as P

MESH = pl.DeviceIdType.MESH
F32 = jnp.float32
BF16 = jnp.bfloat16
W = 128
CH = 4


def flip_matrix():
    row = lax.broadcasted_iota(jnp.int32, (W, W), 0)
    col = lax.broadcasted_iota(jnp.int32, (W, W), 1)
    return jnp.where(row + col == W - 1, 1.0, 0.0).astype(BF16)


def dot(left, right):
    return jnp.dot(left, right, preferred_element_type=F32)


def toeplitz_sum(blocks, row_of, left_of):
    row = lax.broadcasted_iota(jnp.int32, (W, W), 0)
    col = lax.broadcasted_iota(jnp.int32, (W, W), 1)
    lower = row >= col
    before = jnp.zeros((W, W), F32)
    total = None
    for k in range(0, blocks, 2):
        parts = []
        for b in (k, k + 1):
            turned = pltpu.roll(
                jnp.broadcast_to(row_of(b), (W, W)), 1, 1, stride=1, stride_axis=0
            )
            parts.append(jnp.where(lower, turned, before).astype(BF16))
            before = turned
        left = jnp.concatenate([left_of(k), left_of(k + 1)], axis=1)
        term = dot(left, jnp.concatenate(parts, axis=0))
        total = term if total is None else total + term
    return total


def kernel(
    n, scale,
    q_hbm, k_hbm, v_hbm, g_hbm, taps_hbm,
    gated_ref, qgrad_ref, kgrad_ref, vgrad_ref, fgrad_ref,
    q, k, v, g, taps, in_sem,
    send1, recv1, send2, recv2, send3, recv3, sems, all_seq, all_chan,
    tap_rows, tap_flip, wide1, pad_p, pad_x, wide2, wide3,
):
    me_seq = lax.axis_index("seq")
    me_chan = lax.axis_index("chan")
    core = lax.rem(me_seq, 2)
    pair = me_seq + 1 - 2 * core
    late = me_chan >= n // 2

    loads = [
        pltpu.make_async_copy(src, dst, in_sem.at[i])
        for i, (src, dst) in enumerate(
            ((k_hbm, k), (v_hbm, v), (g_hbm, g), (q_hbm, q), (taps_hbm, taps))
        )
    ]
    for load in loads:
        load.start()

    barrier = pltpu.get_barrier_semaphore()

    def tell(sem, **to):
        pl.semaphore_signal(sem, inc=1, device_id=to, device_id_type=MESH)

    def greet_seq(i, carry):
        tell(barrier, seq=lax.rem(me_seq - core + 2 * i, n))
        return carry

    lax.fori_loop(1, n // 2, greet_seq, 0)

    @pl.when(core == 1)
    def _():
        tell(barrier, seq=pair)

    half = lax.broadcasted_iota(jnp.int32, (CH * n // 8, 8, W), 1) < CH
    flip = flip_matrix()

    def swap(x):
        return pltpu.roll(x, CH, 1)

    for load in loads[:4]:
        load.wait()
    tiles = (CH * n // 8, 8, W)
    mixed = (k[...].astype(F32) * v[...].astype(F32)).astype(BF16)
    mixed = dot(mixed, flip).reshape(tiles)
    pulled = (g[...].astype(F32) * q[...].astype(F32)).reshape(tiles)
    paired = jnp.stack(
        [jnp.where(half, mixed, swap(pulled)), jnp.where(half, swap(mixed), pulled)], axis=1
    )
    send1[...] = paired.reshape(n, 8, W).astype(BF16)

    @pl.when(core == 0)
    def _():
        pl.semaphore_wait(barrier, n - 1)
        tell(all_seq, seq=pair)

    @pl.when(core == 1)
    def _():
        pl.semaphore_wait(all_seq, 1)

    def exchange(axis, me, send, recv, at):
        def step(i, carry):
            to = lax.rem(me + i, n)
            pltpu.make_async_remote_copy(
                src_ref=send.at[to], dst_ref=recv.at[me],
                send_sem=sems.at[at], recv_sem=sems.at[at + 1],
                device_id={axis: to}, device_id_type=MESH,
            ).start()
            return carry

        lax.fori_loop(1, n, step, 0)
        recv[me] = send[me]

    def all_of(axis, me, send, recv, at):
        return pltpu.make_async_remote_copy(
            src_ref=send.at[pl.ds(0, n - 1)], dst_ref=recv.at[pl.ds(0, n - 1)],
            send_sem=sems.at[at], recv_sem=sems.at[at + 1],
            device_id={axis: lax.rem(me + 1, n)}, device_id_type=MESH,
        )

    exchange("seq", me_seq, send1, recv1, 0)

    @pl.when(core == 1)
    def _():
        def greet_chan(i, carry):
            tell(barrier, chan=lax.rem(me_chan + i, n))
            return carry

        lax.fori_loop(1, n, greet_chan, 0)

    pad_p[...] = jnp.zeros_like(pad_p)
    pad_x[...] = jnp.zeros_like(pad_x)

    all_of("seq", me_seq, send1, recv1, 0).wait_recv()
    wide1[...] = recv1[...].reshape(n * 8, W).astype(F32)
    for c in range(CH):
        pad_p[c, :n, :] = wide1[pl.ds(CH + c, n, stride=8), :]
        pad_x[c, n:, :] = wide1[pl.ds(c, n, stride=8), :]

    def lags(c, carry):
        wide3[pl.ds(c, n, stride=8), :] = scale * toeplitz_sum(
            n,
            lambda b: pad_x[c, pl.ds(n + b, 1), :],
            lambda b: pad_p[c, b : b + n, :].astype(BF16),
        )
        return carry

    lax.fori_loop(0, CH, lags, 0)
    send3[...] = wide3[...].reshape(n, 8, W)[:, :CH, :]

    def exchange_lags():
        @pl.when(core == 1)
        def _():
            pl.semaphore_wait(barrier, n - 1)
            tell(all_chan, seq=pair)

        @pl.when(core == 0)
        def _():
            pl.semaphore_wait(all_chan, 1)

        exchange("chan", me_chan, send3, recv3, 4)

    pl.when(late)(exchange_lags)

    loads[4].wait()
    tap_values = taps[...].astype(F32)
    for b in range(n):
        tap_rows[CH * b : CH * (b + 1), :] = tap_values[:, W * b : W * (b + 1)]
    tap_flip[...] = dot(tap_rows[...].astype(BF16), flip)

    def convolve(c, carry):
        both = scale * toeplitz_sum(
            n,
            lambda b: tap_flip[pl.ds(CH * b + c, 1), :],
            lambda b: jnp.concatenate(
                [
                    pad_p[c, b : b + n, :].astype(BF16),
                    pad_x[c, n - b : 2 * n - b, :].astype(BF16),
                ],
                axis=0,
            ),
        )
        wide2[pl.ds(c, n, stride=8), :] = both[n:]
        wide2[pl.ds(CH + c, n, stride=8), :] = both[:n]
        return carry

    lax.fori_loop(0, CH, convolve, 0)
    send2[...] = wide2[...].reshape(n, 8, W).astype(BF16)
    exchange("seq", me_seq, send2, recv2, 2)

    all_of("seq", me_seq, send2, recv2, 2).wait_recv()
    came = recv2[...].astype(F32).reshape(CH * n // 8, 2, 8, W)
    low, high = came[:, 0], came[:, 1]
    conv = jnp.where(half, low, swap(high)).reshape(CH * n, W)
    back = jnp.where(half, swap(low), high).reshape(CH * n, W)
    conv = dot(conv.astype(BF16), flip)
    gated_ref[...] = (q[...].astype(F32) * conv).astype(BF16)
    qgrad_ref[...] = (g[...].astype(F32) * conv).astype(BF16)
    kgrad_ref[...] = (back * v[...].astype(F32)).astype(BF16)
    vgrad_ref[...] = (back * k[...].astype(F32)).astype(BF16)

    pl.when(jnp.logical_not(late))(exchange_lags)

    all_of("seq", me_seq, send1, recv1, 0).wait_send()
    all_of("seq", me_seq, send2, recv2, 2).wait_send()
    all_of("chan", me_chan, send3, recv3, 4).wait_send()
    all_of("chan", me_chan, send3, recv3, 4).wait_recv()
    fgrad_ref[...] = jnp.sum(recv3[...], axis=0)


def write_out(*refs):
    count = (len(refs) - 1) // 2
    sem = refs[-1]
    copies = [
        pltpu.make_async_copy(refs[i], refs[count + i], sem.at[i]) for i in range(count)
    ]
    for copy in copies:
        copy.start()
    for copy in copies:
        copy.wait()


def on_device(n, *args):
    rows = CH * n
    length = W * n
    vmem = pl.BlockSpec(memory_space=pltpu.VMEM)
    hbm = pl.BlockSpec(memory_space=pltpu.HBM)
    slab = jax.ShapeDtypeStruct((rows, W), BF16)
    shapes = (slab, slab, slab, slab, jax.ShapeDtypeStruct((CH, W), F32))
    results = pl.pallas_call(
        functools.partial(kernel, n, 1.0 / math.sqrt(length)),
        out_shape=shapes,
        in_specs=[hbm] * 5,
        out_specs=(vmem,) * 5,
        scratch_shapes=[pltpu.VMEM((rows, W), BF16)] * 4
        + [
            pltpu.VMEM((CH, length), BF16),
            pltpu.SemaphoreType.DMA((5,)),
            pltpu.VMEM((n, 8, W), BF16),
            pltpu.VMEM((n, 8, W), BF16),
            pltpu.VMEM((n, 8, W), BF16),
            pltpu.VMEM((n, 8, W), BF16),
            pltpu.VMEM((n, CH, W), F32),
            pltpu.VMEM((n, CH, W), F32),
            pltpu.SemaphoreType.DMA((6,)),
            pltpu.SemaphoreType.REGULAR,
            pltpu.SemaphoreType.REGULAR,
            pltpu.VMEM((rows, W), F32),
            pltpu.VMEM((rows, W), F32),
            pltpu.VMEM((8 * n, W), F32),
            pltpu.VMEM((CH, 2 * n, W), F32),
            pltpu.VMEM((CH, 2 * n, W), F32),
            pltpu.VMEM((8 * n, W), F32),
            pltpu.VMEM((8 * n, W), F32),
        ],
        compiler_params=pltpu.CompilerParams(
            collective_id=0, has_side_effects=True, vmem_limit_bytes=32 << 20
        ),
    )(*(pltpu.with_memory_space_constraint(x, pltpu.HBM) for x in args))
    return pl.pallas_call(
        write_out,
        out_shape=shapes,
        in_specs=[vmem] * 5,
        out_specs=(hbm,) * 5,
        scratch_shapes=[pltpu.SemaphoreType.DMA((5,))],
    )(*(pltpu.with_memory_space_constraint(x, pltpu.VMEM) for x in results))


def solution(mesh):
    return jax.shard_map(
        functools.partial(on_device, mesh.shape["seq"]),
        mesh=mesh,
        in_specs=(
            P("chan", "seq"),
            P("chan", "seq"),
            P("chan", "seq"),
            P("chan", "seq"),
            P("seq", None),
        ),
        out_specs=(
            P("chan", "seq"),
            P("chan", "seq"),
            P("chan", "seq"),
            P("chan", "seq"),
            P("seq", "chan"),
        ),
        check_vma=False,
    )
```

```python
import functools
import math

import jax
import jax.numpy as jnp
from jax import lax
from jax.experimental import pallas as pl
from jax.experimental.pallas import tpu as pltpu
from jax.sharding import PartitionSpec as P

MESH = pl.DeviceIdType.MESH
F32 = jnp.float32
BF16 = jnp.bfloat16
W = 128
CH = 4


def flip_matrix():
    row = lax.broadcasted_iota(jnp.int32, (W, W), 0)
    col = lax.broadcasted_iota(jnp.int32, (W, W), 1)
    return jnp.where(row + col == W - 1, 1.0, 0.0).astype(BF16)


def dot(left, right):
    return jnp.dot(left, right, preferred_element_type=F32)


def toeplitz_sum(blocks, row_of, left_of):
    row = lax.broadcasted_iota(jnp.int32, (W, W), 0)
    col = lax.broadcasted_iota(jnp.int32, (W, W), 1)
    lower = row >= col
    before = jnp.zeros((W, W), F32)
    total = None
    for k in range(0, blocks, 2):
        parts = []
        for b in (k, k + 1):
            turned = pltpu.roll(
                jnp.broadcast_to(row_of(b), (W, W)), 1, 1, stride=1, stride_axis=0
            )
            parts.append(jnp.where(lower, turned, before).astype(BF16))
            before = turned
        left = jnp.concatenate([left_of(k), left_of(k + 1)], axis=1)
        term = dot(left, jnp.concatenate(parts, axis=0))
        total = term if total is None else total + term
    return total


def kernel(
    n, scale,
    q_hbm, k_hbm, v_hbm, g_hbm, taps_hbm,
    gated_ref, qgrad_ref, kgrad_ref, vgrad_ref, fgrad_ref,
    q, k, v, g, taps, in_sem,
    send1, recv1, send2, recv2, send3, recv3, sems, all_seq, all_chan,
    tap_rows, tap_flip, wide1, pad_p, pad_x, wide2, wide3,
):
    me_seq = lax.axis_index("seq")
    me_chan = lax.axis_index("chan")
    core = lax.rem(me_seq, 2)
    pair = me_seq + 1 - 2 * core
    late = me_chan >= n // 2

    loads = [
        pltpu.make_async_copy(src, dst, in_sem.at[i])
        for i, (src, dst) in enumerate(
            ((k_hbm, k), (v_hbm, v), (g_hbm, g), (q_hbm, q), (taps_hbm, taps))
        )
    ]
    for load in loads:
        load.start()

    barrier = pltpu.get_barrier_semaphore()

    def tell(sem, **to):
        pl.semaphore_signal(sem, inc=1, device_id=to, device_id_type=MESH)

    chips = n // 2
    outer = min(chips, 4)
    inner = chips // outer
    own = (inner // 2) * outer + outer // 2
    my_outer, my_inner = me_seq // (2 * inner), lax.rem(me_seq // 2, inner)

    def chip_at(i):
        at_outer = lax.rem(my_outer + outer // 2 + lax.rem(i, outer), outer)
        at_inner = lax.rem(my_inner + inner // 2 + i // outer, inner)
        return 2 * (at_outer * inner + at_inner)

    def each_other_chip(step):
        def body(i, carry):
            step(chip_at(i))
            return carry

        lax.fori_loop(0, own, body, 0)
        lax.fori_loop(own + 1, chips, body, 0)

    each_other_chip(lambda to: tell(barrier, seq=to))

    @pl.when(core == 1)
    def _():
        tell(barrier, seq=pair)

    def greet_chan(i, carry):
        tell(barrier, seq=me_seq - core + 1, chan=i)
        return carry

    lax.fori_loop(0, me_chan, greet_chan, 0)
    lax.fori_loop(me_chan + 1, n, greet_chan, 0)

    half = lax.broadcasted_iota(jnp.int32, (CH * n // 8, 8, W), 1) < CH
    flip = flip_matrix()

    def swap(x):
        return pltpu.roll(x, CH, 1)

    for load in loads[:4]:
        load.wait()
    tiles = (CH * n // 8, 8, W)
    mixed = (k[...].astype(F32) * v[...].astype(F32)).astype(BF16)
    mixed = dot(mixed, flip).reshape(tiles)
    pulled = (g[...].astype(F32) * q[...].astype(F32)).reshape(tiles)
    paired = jnp.stack(
        [jnp.where(half, mixed, swap(pulled)), jnp.where(half, swap(mixed), pulled)], axis=1
    )
    send1[...] = paired.reshape(n, 8, W).astype(BF16)

    @pl.when(core == 0)
    def _():
        pl.semaphore_wait(barrier, n - 1)
        tell(all_seq, seq=pair)

    @pl.when(core == 1)
    def _():
        pl.semaphore_wait(all_seq, 1)

    def send_one(axis, me, to, send, recv, at):
        pltpu.make_async_remote_copy(
            src_ref=send.at[to], dst_ref=recv.at[me],
            send_sem=sems.at[at], recv_sem=sems.at[at + 1],
            device_id={axis: to}, device_id_type=MESH,
        ).start()

    def exchange_seq(send, recv, at):
        def both_cores(to):
            send_one("seq", me_seq, to, send, recv, at)
            send_one("seq", me_seq, to + 1, send, recv, at)

        each_other_chip(both_cores)
        send_one("seq", me_seq, pair, send, recv, at)
        recv[me_seq] = send[me_seq]

    def exchange_chan(send, recv, at):
        def step(i, carry):
            send_one("chan", me_chan, i, send, recv, at)
            return carry

        lax.fori_loop(0, me_chan, step, 0)
        lax.fori_loop(me_chan + 1, n, step, 0)
        recv[me_chan] = send[me_chan]

    def all_of(axis, me, send, recv, at):
        return pltpu.make_async_remote_copy(
            src_ref=send.at[pl.ds(0, n - 1)], dst_ref=recv.at[pl.ds(0, n - 1)],
            send_sem=sems.at[at], recv_sem=sems.at[at + 1],
            device_id={axis: lax.rem(me + 1, n)}, device_id_type=MESH,
        )

    exchange_seq(send1, recv1, 0)

    pad_p[...] = jnp.zeros_like(pad_p)
    pad_x[...] = jnp.zeros_like(pad_x)

    all_of("seq", me_seq, send1, recv1, 0).wait_recv()
    wide1[...] = recv1[...].reshape(n * 8, W).astype(F32)
    for c in range(CH):
        pad_p[c, :n, :] = wide1[pl.ds(CH + c, n, stride=8), :]
        pad_x[c, n:, :] = wide1[pl.ds(c, n, stride=8), :]

    for c in range(CH):
        wide3[pl.ds(c, n, stride=8), :] = scale * toeplitz_sum(
            n,
            lambda b: pad_x[c, pl.ds(n + b, 1), :],
            lambda b: pad_p[c, b : b + n, :].astype(BF16),
        )
    send3[...] = wide3[...].reshape(n, 8, W)[:, :CH, :]

    def exchange_lags():
        @pl.when(core == 1)
        def _():
            pl.semaphore_wait(barrier, 2 * (n - 1))
            tell(all_chan, seq=pair)

        @pl.when(core == 0)
        def _():
            pl.semaphore_wait(all_chan, 1)

        exchange_chan(send3, recv3, 4)

    pl.when(late)(exchange_lags)

    loads[4].wait()
    tap_values = taps[...].astype(F32)
    for b in range(n):
        tap_rows[CH * b : CH * (b + 1), :] = tap_values[:, W * b : W * (b + 1)]
    tap_flip[...] = dot(tap_rows[...].astype(BF16), flip)

    for c in range(CH):
        both = scale * toeplitz_sum(
            n,
            lambda b: tap_flip[pl.ds(CH * b + c, 1), :],
            lambda b: jnp.concatenate(
                [
                    pad_p[c, b : b + n, :].astype(BF16),
                    pad_x[c, n - b : 2 * n - b, :].astype(BF16),
                ],
                axis=0,
            ),
        )
        wide2[pl.ds(c, n, stride=8), :] = both[n:]
        wide2[pl.ds(CH + c, n, stride=8), :] = both[:n]
    send2[...] = wide2[...].reshape(n, 8, W).astype(BF16)
    exchange_seq(send2, recv2, 2)
    pl.when(jnp.logical_not(late))(exchange_lags)

    all_of("seq", me_seq, send2, recv2, 2).wait_recv()
    came = recv2[...].astype(F32).reshape(CH * n // 8, 2, 8, W)
    low, high = came[:, 0], came[:, 1]
    conv = jnp.where(half, low, swap(high)).reshape(CH * n, W)
    back = jnp.where(half, swap(low), high).reshape(CH * n, W)
    conv = dot(conv.astype(BF16), flip)
    gated_ref[...] = (q[...].astype(F32) * conv).astype(BF16)
    qgrad_ref[...] = (g[...].astype(F32) * conv).astype(BF16)
    kgrad_ref[...] = (back * v[...].astype(F32)).astype(BF16)
    vgrad_ref[...] = (back * k[...].astype(F32)).astype(BF16)

    all_of("seq", me_seq, send1, recv1, 0).wait_send()
    all_of("seq", me_seq, send2, recv2, 2).wait_send()
    all_of("chan", me_chan, send3, recv3, 4).wait_send()
    all_of("chan", me_chan, send3, recv3, 4).wait_recv()
    fgrad_ref[...] = jnp.sum(recv3[...], axis=0)


def write_out(*refs):
    count = (len(refs) - 1) // 2
    sem = refs[-1]
    copies = [
        pltpu.make_async_copy(refs[i], refs[count + i], sem.at[i]) for i in range(count)
    ]
    for copy in copies:
        copy.start()
    for copy in copies:
        copy.wait()


def on_device(n, *args):
    rows = CH * n
    length = W * n
    vmem = pl.BlockSpec(memory_space=pltpu.VMEM)
    hbm = pl.BlockSpec(memory_space=pltpu.HBM)
    slab = jax.ShapeDtypeStruct((rows, W), BF16)
    shapes = (slab, slab, slab, slab, jax.ShapeDtypeStruct((CH, W), F32))
    results = pl.pallas_call(
        functools.partial(kernel, n, 1.0 / math.sqrt(length)),
        out_shape=shapes,
        in_specs=[hbm] * 5,
        out_specs=(vmem,) * 5,
        scratch_shapes=[pltpu.VMEM((rows, W), BF16)] * 4
        + [
            pltpu.VMEM((CH, length), BF16),
            pltpu.SemaphoreType.DMA((5,)),
            pltpu.VMEM((n, 8, W), BF16),
            pltpu.VMEM((n, 8, W), BF16),
            pltpu.VMEM((n, 8, W), BF16),
            pltpu.VMEM((n, 8, W), BF16),
            pltpu.VMEM((n, CH, W), F32),
            pltpu.VMEM((n, CH, W), F32),
            pltpu.SemaphoreType.DMA((6,)),
            pltpu.SemaphoreType.REGULAR,
            pltpu.SemaphoreType.REGULAR,
            pltpu.VMEM((rows, W), F32),
            pltpu.VMEM((rows, W), F32),
            pltpu.VMEM((8 * n, W), F32),
            pltpu.VMEM((CH, 2 * n, W), F32),
            pltpu.VMEM((CH, 2 * n, W), F32),
            pltpu.VMEM((8 * n, W), F32),
            pltpu.VMEM((8 * n, W), F32),
        ],
        compiler_params=pltpu.CompilerParams(
            collective_id=0, has_side_effects=True, vmem_limit_bytes=32 << 20
        ),
    )(*(pltpu.with_memory_space_constraint(x, pltpu.HBM) for x in args))
    return pl.pallas_call(
        write_out,
        out_shape=shapes,
        in_specs=[vmem] * 5,
        out_specs=(hbm,) * 5,
        scratch_shapes=[pltpu.SemaphoreType.DMA((5,))],
    )(*(pltpu.with_memory_space_constraint(x, pltpu.VMEM) for x in results))


def solution(mesh):
    return jax.shard_map(
        functools.partial(on_device, mesh.shape["seq"]),
        mesh=mesh,
        in_specs=(
            P("chan", "seq"),
            P("chan", "seq"),
            P("chan", "seq"),
            P("chan", "seq"),
            P("seq", None),
        ),
        out_specs=(
            P("chan", "seq"),
            P("chan", "seq"),
            P("chan", "seq"),
            P("chan", "seq"),
            P("seq", "chan"),
        ),
        check_vma=False,
    )
```

```python
import functools
import math

import jax
import jax.numpy as jnp
from jax import lax
from jax.experimental import pallas as pl
from jax.experimental.pallas import tpu as pltpu
from jax.sharding import PartitionSpec as P

MESH = pl.DeviceIdType.MESH
F32 = jnp.float32
BF16 = jnp.bfloat16
W = 128
CH = 4


def flip_matrix():
    row = lax.broadcasted_iota(jnp.int32, (W, W), 0)
    col = lax.broadcasted_iota(jnp.int32, (W, W), 1)
    return jnp.where(row + col == W - 1, 1.0, 0.0).astype(BF16)


def dot(left, right):
    return jnp.dot(left, right, preferred_element_type=F32)


def toeplitz_sum(blocks, row_of, left_of):
    row = lax.broadcasted_iota(jnp.int32, (W, W), 0)
    col = lax.broadcasted_iota(jnp.int32, (W, W), 1)
    lower = row >= col
    before = jnp.zeros((W, W), F32)
    total = None
    for k in range(0, blocks, 2):
        parts = []
        for b in (k, k + 1):
            turned = pltpu.roll(
                jnp.broadcast_to(row_of(b), (W, W)), 1, 1, stride=1, stride_axis=0
            )
            parts.append(jnp.where(lower, turned, before).astype(BF16))
            before = turned
        left = jnp.concatenate([left_of(k), left_of(k + 1)], axis=1)
        term = dot(left, jnp.concatenate(parts, axis=0))
        total = term if total is None else total + term
    return total


def kernel(
    n, scale,
    q_hbm, k_hbm, v_hbm, g_hbm, taps_hbm,
    gated_ref, qgrad_ref, kgrad_ref, vgrad_ref, fgrad_ref,
    q, k, v, g, taps, in_sem,
    send1, recv1, send2, recv2, send3, recv3, sems, all_seq, all_chan,
    tap_rows, tap_flip, wide1, pad_p, pad_x, wide2, wide3,
):
    me_seq = lax.axis_index("seq")
    me_chan = lax.axis_index("chan")
    core = lax.rem(me_seq, 2)
    pair = me_seq + 1 - 2 * core
    lags_turn = jnp.where(me_chan >= 3 * n // 8, 0, 1)
    last = me_chan >= 3 * n // 4

    barrier = pltpu.get_barrier_semaphore()

    def tell(sem, **to):
        pl.semaphore_signal(sem, inc=1, device_id=to, device_id_type=MESH)

    chips = n // 2
    outer = min(chips, 4)
    inner = chips // outer
    own = (inner // 2) * outer + outer // 2
    my_outer, my_inner = me_seq // (2 * inner), lax.rem(me_seq // 2, inner)

    def chip_at(i):
        at_outer = lax.rem(my_outer + outer // 2 + lax.rem(i, outer), outer)
        at_inner = lax.rem(my_inner + inner // 2 + i // outer, inner)
        return 2 * (at_outer * inner + at_inner)

    def each_other_chip(step):
        def body(i, carry):
            step(chip_at(i))
            return carry

        lax.fori_loop(0, own, body, 0)
        lax.fori_loop(own + 1, chips, body, 0)

    each_other_chip(lambda to: tell(barrier, seq=to))

    @pl.when(core == 1)
    def _():
        tell(barrier, seq=pair)

    loads = [
        pltpu.make_async_copy(src, dst, in_sem.at[i])
        for i, (src, dst) in enumerate(
            ((k_hbm, k), (v_hbm, v), (g_hbm, g), (q_hbm, q), (taps_hbm, taps))
        )
    ]
    for load in loads:
        load.start()

    def greet_chan(i, carry):
        tell(barrier, seq=me_seq - core + 1, chan=i)
        return carry

    lax.fori_loop(0, me_chan, greet_chan, 0)
    lax.fori_loop(me_chan + 1, n, greet_chan, 0)

    half = lax.broadcasted_iota(jnp.int32, (CH * n // 8, 8, W), 1) < CH
    flip = flip_matrix()

    def swap(x):
        return pltpu.roll(x, CH, 1)

    for load in loads[:4]:
        load.wait()
    tiles = (CH * n // 8, 8, W)
    mixed = (k[...].astype(F32) * v[...].astype(F32)).astype(BF16)
    mixed = dot(mixed, flip).reshape(tiles)
    pulled = (g[...].astype(F32) * q[...].astype(F32)).reshape(tiles)
    paired = jnp.stack(
        [jnp.where(half, mixed, swap(pulled)), jnp.where(half, swap(mixed), pulled)], axis=1
    )
    send1[...] = paired.reshape(n, 8, W).astype(BF16)

    @pl.when(core == 0)
    def _():
        pl.semaphore_wait(barrier, n - 1)
        tell(all_seq, seq=pair)

    @pl.when(core == 1)
    def _():
        pl.semaphore_wait(all_seq, 1)

    def send_one(axis, me, to, send, recv, at):
        pltpu.make_async_remote_copy(
            src_ref=send.at[to], dst_ref=recv.at[me],
            send_sem=sems.at[at], recv_sem=sems.at[at + 1],
            device_id={axis: to}, device_id_type=MESH,
        ).start()

    def exchange_seq(send, recv, at):
        def both_cores(to):
            send_one("seq", me_seq, to, send, recv, at)
            send_one("seq", me_seq, to + 1, send, recv, at)

        each_other_chip(both_cores)
        send_one("seq", me_seq, pair, send, recv, at)
        recv[me_seq] = send[me_seq]

    def exchange_chan(send, recv, at):
        def step(i, carry):
            send_one("chan", me_chan, i, send, recv, at)
            return carry

        lax.fori_loop(0, me_chan, step, 0)
        lax.fori_loop(me_chan + 1, n, step, 0)
        recv[me_chan] = send[me_chan]

    def all_of(axis, me, send, recv, at):
        return pltpu.make_async_remote_copy(
            src_ref=send.at[pl.ds(0, n - 1)], dst_ref=recv.at[pl.ds(0, n - 1)],
            send_sem=sems.at[at], recv_sem=sems.at[at + 1],
            device_id={axis: lax.rem(me + 1, n)}, device_id_type=MESH,
        )

    exchange_seq(send1, recv1, 0)

    pad_p[...] = jnp.zeros_like(pad_p)
    pad_x[...] = jnp.zeros_like(pad_x)

    loads[4].wait()
    tap_values = taps[...].astype(F32)
    for b in range(n):
        tap_rows[CH * b : CH * (b + 1), :] = tap_values[:, W * b : W * (b + 1)]
    tap_flip[...] = dot(tap_rows[...].astype(BF16), flip)

    all_of("seq", me_seq, send1, recv1, 0).wait_recv()
    wide1[...] = recv1[...].reshape(n * 8, W).astype(F32)
    for c in range(CH):
        pad_p[c, :n, :] = wide1[pl.ds(CH + c, n, stride=8), :]
        pad_x[c, n:, :] = wide1[pl.ds(c, n, stride=8), :]

    def pass_chan_on():
        @pl.when(core == 1)
        def _():
            pl.semaphore_wait(barrier, 2 * (n - 1))
            tell(all_chan, seq=pair)

    def lags():
        for c in range(CH):
            wide3[pl.ds(c, n, stride=8), :] = scale * toeplitz_sum(
                n,
                lambda b: pad_x[c, pl.ds(n + b, 1), :],
                lambda b: pad_p[c, b : b + n, :].astype(BF16),
            )
        send3[...] = wide3[...].reshape(n, 8, W)[:, :CH, :]
        pl.when(jnp.logical_not(last))(pass_chan_on)

        @pl.when(core == 0)
        def _():
            pl.semaphore_wait(all_chan, 1)

        exchange_chan(send3, recv3, 4)

    def convolutions():
        for c in range(CH):
            both = scale * toeplitz_sum(
                n,
                lambda b: tap_flip[pl.ds(CH * b + c, 1), :],
                lambda b: jnp.concatenate(
                    [
                        pad_p[c, b : b + n, :].astype(BF16),
                        pad_x[c, n - b : 2 * n - b, :].astype(BF16),
                    ],
                    axis=0,
                ),
            )
            wide2[pl.ds(c, n, stride=8), :] = both[n:]
            wide2[pl.ds(CH + c, n, stride=8), :] = both[:n]
        send2[...] = wide2[...].reshape(n, 8, W).astype(BF16)
        exchange_seq(send2, recv2, 2)

    pl.when(last)(pass_chan_on)

    def turn(i, carry):
        pl.when(i == lags_turn)(lags)
        pl.when(i != lags_turn)(convolutions)
        return carry

    lax.fori_loop(0, 2, turn, 0)

    all_of("seq", me_seq, send2, recv2, 2).wait_recv()
    came = recv2[...].astype(F32).reshape(CH * n // 8, 2, 8, W)
    low, high = came[:, 0], came[:, 1]
    conv = jnp.where(half, low, swap(high)).reshape(CH * n, W)
    back = jnp.where(half, swap(low), high).reshape(CH * n, W)
    conv = dot(conv.astype(BF16), flip)
    gated_ref[...] = (q[...].astype(F32) * conv).astype(BF16)
    qgrad_ref[...] = (g[...].astype(F32) * conv).astype(BF16)
    kgrad_ref[...] = (back * v[...].astype(F32)).astype(BF16)
    vgrad_ref[...] = (back * k[...].astype(F32)).astype(BF16)

    all_of("seq", me_seq, send1, recv1, 0).wait_send()
    all_of("seq", me_seq, send2, recv2, 2).wait_send()
    all_of("chan", me_chan, send3, recv3, 4).wait_send()
    all_of("chan", me_chan, send3, recv3, 4).wait_recv()
    fgrad_ref[...] = jnp.sum(recv3[...], axis=0)


def write_out(*refs):
    count = (len(refs) - 1) // 2
    sem = refs[-1]
    copies = [
        pltpu.make_async_copy(refs[i], refs[count + i], sem.at[i]) for i in range(count)
    ]
    for copy in copies:
        copy.start()
    for copy in copies:
        copy.wait()


def on_device(n, *args):
    rows = CH * n
    length = W * n
    vmem = pl.BlockSpec(memory_space=pltpu.VMEM)
    hbm = pl.BlockSpec(memory_space=pltpu.HBM)
    slab = jax.ShapeDtypeStruct((rows, W), BF16)
    shapes = (slab, slab, slab, slab, jax.ShapeDtypeStruct((CH, W), F32))
    results = pl.pallas_call(
        functools.partial(kernel, n, 1.0 / math.sqrt(length)),
        out_shape=shapes,
        in_specs=[hbm] * 5,
        out_specs=(vmem,) * 5,
        scratch_shapes=[pltpu.VMEM((rows, W), BF16)] * 4
        + [
            pltpu.VMEM((CH, length), BF16),
            pltpu.SemaphoreType.DMA((5,)),
            pltpu.VMEM((n, 8, W), BF16),
            pltpu.VMEM((n, 8, W), BF16),
            pltpu.VMEM((n, 8, W), BF16),
            pltpu.VMEM((n, 8, W), BF16),
            pltpu.VMEM((n, CH, W), F32),
            pltpu.VMEM((n, CH, W), F32),
            pltpu.SemaphoreType.DMA((6,)),
            pltpu.SemaphoreType.REGULAR,
            pltpu.SemaphoreType.REGULAR,
            pltpu.VMEM((rows, W), F32),
            pltpu.VMEM((rows, W), F32),
            pltpu.VMEM((8 * n, W), F32),
            pltpu.VMEM((CH, 2 * n, W), F32),
            pltpu.VMEM((CH, 2 * n, W), F32),
            pltpu.VMEM((8 * n, W), F32),
            pltpu.VMEM((8 * n, W), F32),
        ],
        compiler_params=pltpu.CompilerParams(
            collective_id=0, has_side_effects=True, vmem_limit_bytes=32 << 20
        ),
    )(*(pltpu.with_memory_space_constraint(x, pltpu.HBM) for x in args))
    return pl.pallas_call(
        write_out,
        out_shape=shapes,
        in_specs=[vmem] * 5,
        out_specs=(hbm,) * 5,
        scratch_shapes=[pltpu.SemaphoreType.DMA((5,))],
    )(*(pltpu.with_memory_space_constraint(x, pltpu.VMEM) for x in results))


def solution(mesh):
    return jax.shard_map(
        functools.partial(on_device, mesh.shape["seq"]),
        mesh=mesh,
        in_specs=(
            P("chan", "seq"),
            P("chan", "seq"),
            P("chan", "seq"),
            P("chan", "seq"),
            P("seq", None),
        ),
        out_specs=(
            P("chan", "seq"),
            P("chan", "seq"),
            P("chan", "seq"),
            P("chan", "seq"),
            P("seq", "chan"),
        ),
        check_vma=False,
    )
```

```python
import functools
import math

import jax
import jax.numpy as jnp
from jax import lax
from jax.experimental import pallas as pl
from jax.experimental.pallas import tpu as pltpu
from jax.sharding import PartitionSpec as P

MESH = pl.DeviceIdType.MESH
F32 = jnp.float32
BF16 = jnp.bfloat16
W = 128
G = 32
CH = 4


def flip_matrix():
    row = lax.broadcasted_iota(jnp.int32, (W, W), 0)
    col = lax.broadcasted_iota(jnp.int32, (W, W), 1)
    return jnp.where(row + col == W - 1, 1.0, 0.0).astype(BF16)


def dot(left, right):
    return jnp.dot(left, right, preferred_element_type=F32)


def toeplitz_sum(blocks, row_of, left_of):
    row = lax.broadcasted_iota(jnp.int32, (W, W), 0)
    col = lax.broadcasted_iota(jnp.int32, (W, W), 1)
    lower = row >= col
    before = jnp.zeros((W, W), F32)
    total = None
    for k in range(0, blocks, 2):
        parts = []
        for b in (k, k + 1):
            turned = pltpu.roll(
                jnp.broadcast_to(row_of(b), (W, W)), 1, 1, stride=1, stride_axis=0
            )
            parts.append(jnp.where(lower, turned, before).astype(BF16))
            before = turned
        left = jnp.concatenate([left_of(k), left_of(k + 1)], axis=1)
        term = dot(left, jnp.concatenate(parts, axis=0))
        total = term if total is None else total + term
    return total


def shifted_rows(rows_of, turned):
    lane = lax.broadcasted_iota(jnp.int32, (rows_of, W), 1)
    return [
        jnp.where(
            lane < 2 * G,
            jnp.where(lane < G, turned(-r % 4, 0), turned((1 - r) % 4, 1)),
            jnp.where(lane < 3 * G, turned((2 - r) % 4, 2), turned((3 - r) % 4, 3)),
        )
        for r in range(4)
    ]


def lag_sum(blocks, row_of, left_of):
    row = lax.broadcasted_iota(jnp.int32, (G, W), 0)
    col = lax.broadcasted_iota(jnp.int32, (G, W), 1)
    lower = row >= col
    before = jnp.zeros((G, W), F32)
    bases = []
    for k in range(blocks + 1):
        if k < blocks:
            turned = pltpu.roll(
                jnp.broadcast_to(row_of(k), (G, W)), 1, 1, stride=1, stride_axis=0
            )
        else:
            turned = jnp.zeros((G, W), F32)
        bases.append(jnp.where(lower, turned, before).astype(BF16))
        before = turned
    total = None
    step = min(blocks, 8)
    for k in range(0, blocks, step):
        right = jnp.concatenate(
            [jnp.concatenate([bases[b + 1], bases[b]], axis=1) for b in range(k, k + step)], axis=0
        )
        left = jnp.concatenate([left_of(t) for t in range(k // 4, (k + step) // 4)], axis=1)
        term = dot(left, right)
        total = term if total is None else total + term
    lane = lax.broadcasted_iota(jnp.int32, (blocks, W), 1)
    out = total[:blocks, W:]
    for r in range(1, 4):
        part = total[r * blocks : (r + 1) * blocks]
        chosen = jnp.where(lane < W - G * r, part[:, W:], part[:, :W])
        out = out + pltpu.roll(chosen, G * r, 1)
    return out


def kernel(
    n, scale,
    q_hbm, k_hbm, v_hbm, g_hbm, taps_hbm,
    gated_ref, qgrad_ref, kgrad_ref, vgrad_ref, fgrad_ref,
    q, k, v, g, taps, in_sem,
    send1, recv1, send2, recv2, send3, recv3, sems, all_seq, all_chan,
    tap_rows, tap_flip, wide1, pad_p, pad_x, wide2, wide3, turned_p, pad_q,
):
    me_seq = lax.axis_index("seq")
    me_chan = lax.axis_index("chan")
    core = lax.rem(me_seq, 2)
    pair = me_seq + 1 - 2 * core
    lags_turn = jnp.where(me_chan >= 3 * n // 8, 0, 1)

    barrier = pltpu.get_barrier_semaphore()

    def tell(sem, **to):
        pl.semaphore_signal(sem, inc=1, device_id=to, device_id_type=MESH)

    chips = n // 2
    outer = min(chips, 4)
    inner = chips // outer
    own = (inner // 2) * outer + outer // 2
    my_outer, my_inner = me_seq // (2 * inner), lax.rem(me_seq // 2, inner)

    def chip_at(i):
        at_outer = lax.rem(my_outer + outer // 2 + lax.rem(i, outer), outer)
        at_inner = lax.rem(my_inner + inner // 2 + i // outer, inner)
        return 2 * (at_outer * inner + at_inner)

    def each_other_chip(step):
        def body(i, carry):
            step(chip_at(i))
            return carry

        lax.fori_loop(0, own, body, 0)
        lax.fori_loop(own + 1, chips, body, 0)

    each_other_chip(lambda to: tell(barrier, seq=to))

    @pl.when(core == 1)
    def _():
        tell(barrier, seq=pair)

    loads = [
        pltpu.make_async_copy(src, dst, in_sem.at[i])
        for i, (src, dst) in enumerate(
            ((k_hbm, k), (v_hbm, v), (g_hbm, g), (q_hbm, q), (taps_hbm, taps))
        )
    ]
    for load in loads:
        load.start()

    def greet_chan(i, carry):
        @pl.when(i != me_chan)
        def _():
            tell(barrier, seq=me_seq - core + 1, chan=i)

        return carry

    lax.fori_loop(n // 4, 3 * n // 4, greet_chan, 0)

    half = lax.broadcasted_iota(jnp.int32, (CH * n // 8, 8, W), 1) < CH
    flip = flip_matrix()

    def swap(x):
        return pltpu.roll(x, CH, 1)

    for load in loads[:4]:
        load.wait()
    tiles = (CH * n // 8, 8, W)
    mixed = (k[...].astype(F32) * v[...].astype(F32)).astype(BF16)
    mixed = dot(mixed, flip).reshape(tiles)
    pulled = (g[...].astype(F32) * q[...].astype(F32)).reshape(tiles)
    paired = jnp.stack(
        [jnp.where(half, mixed, swap(pulled)), jnp.where(half, swap(mixed), pulled)], axis=1
    )
    send1[...] = paired.reshape(n, 8, W).astype(BF16)

    @pl.when(core == 0)
    def _():
        pl.semaphore_wait(barrier, n - 1)
        tell(all_seq, seq=pair)

    @pl.when(core == 1)
    def _():
        pl.semaphore_wait(all_seq, 1)

    def send_one(axis, me, to, send, recv, at):
        pltpu.make_async_remote_copy(
            src_ref=send.at[to], dst_ref=recv.at[me],
            send_sem=sems.at[at], recv_sem=sems.at[at + 1],
            device_id={axis: to}, device_id_type=MESH,
        ).start()

    def exchange_seq(send, recv, at):
        def both_cores(to):
            send_one("seq", me_seq, to, send, recv, at)
            send_one("seq", me_seq, to + 1, send, recv, at)

        each_other_chip(both_cores)
        send_one("seq", me_seq, pair, send, recv, at)
        recv[me_seq] = send[me_seq]

    def exchange_chan(send, recv, at):
        def step(i, carry):
            send_one("chan", me_chan, i, send, recv, at)
            return carry

        lax.fori_loop(0, me_chan, step, 0)
        lax.fori_loop(me_chan + 1, n, step, 0)
        recv[me_chan] = send[me_chan]

    def all_of(axis, me, send, recv, at):
        return pltpu.make_async_remote_copy(
            src_ref=send.at[pl.ds(0, n - 1)], dst_ref=recv.at[pl.ds(0, n - 1)],
            send_sem=sems.at[at], recv_sem=sems.at[at + 1],
            device_id={axis: lax.rem(me + 1, n)}, device_id_type=MESH,
        )

    exchange_seq(send1, recv1, 0)
    lax.fori_loop(0, n // 4, greet_chan, 0)
    lax.fori_loop(3 * n // 4, n, greet_chan, 0)

    pad_p[...] = jnp.zeros_like(pad_p)
    pad_x[...] = jnp.zeros_like(pad_x)
    pad_q[...] = jnp.zeros_like(pad_q)
    turned_p[...] = jnp.zeros_like(turned_p)

    loads[4].wait()
    tap_values = taps[...].astype(F32)
    for b in range(n):
        tap_rows[CH * b : CH * (b + 1), :] = tap_values[:, W * b : W * (b + 1)]
    tap_flip[...] = dot(tap_rows[...].astype(BF16), flip)

    all_of("seq", me_seq, send1, recv1, 0).wait_recv()
    wide1[...] = recv1[...].reshape(n * 8, W).astype(F32)
    for c in range(CH):
        pad_p[c, :n, :] = wide1[pl.ds(CH + c, n, stride=8), :]
        pad_x[c, n:, :] = wide1[pl.ds(c, n, stride=8), :]

    def pass_chan_on():
        @pl.when(core == 1)
        def _():
            pl.semaphore_wait(barrier, 2 * (n - 1))
            tell(all_chan, seq=pair)

    def lags():
        pass_chan_on()
        for c in range(CH):
            for s in range(4):
                own_rows = pad_p[c, :n, :]
                turned_p[s, c, :n, :] = pltpu.roll(own_rows, G * s, 1) if s else own_rows
        for c in range(CH):
            for r, rows in enumerate(
                shifted_rows(n, lambda s, j: turned_p[s, c, j : j + n, :])
            ):
                pad_q[c, r, :n, :] = rows
            wide3[pl.ds(c, n, stride=8), :] = scale * lag_sum(
                n,
                lambda b: pad_x[c, pl.ds(n + b, 1), :],
                lambda t: jnp.concatenate(
                    [pad_q[c, r, 4 * t : 4 * t + n, :].astype(BF16) for r in range(4)], axis=0
                ),
            )
        send3[...] = wide3[...].reshape(n, 8, W)[:, :CH, :]
        @pl.when(core == 0)
        def _():
            pl.semaphore_wait(all_chan, 1)

        exchange_chan(send3, recv3, 4)

    def convolutions():
        for c in range(CH):
            both = scale * toeplitz_sum(
                n,
                lambda b: tap_flip[pl.ds(CH * b + c, 1), :],
                lambda b: jnp.concatenate(
                    [
                        pad_p[c, b : b + n, :].astype(BF16),
                        pad_x[c, n - b : 2 * n - b, :].astype(BF16),
                    ],
                    axis=0,
                ),
            )
            wide2[pl.ds(c, n, stride=8), :] = both[n:]
            wide2[pl.ds(CH + c, n, stride=8), :] = both[:n]
        send2[...] = wide2[...].reshape(n, 8, W).astype(BF16)
        exchange_seq(send2, recv2, 2)

    def turn(i, carry):
        pl.when(i == lags_turn)(lags)
        pl.when(i != lags_turn)(convolutions)
        return carry

    lax.fori_loop(0, 2, turn, 0)

    all_of("seq", me_seq, send2, recv2, 2).wait_recv()
    came = recv2[...].astype(F32).reshape(CH * n // 8, 2, 8, W)
    low, high = came[:, 0], came[:, 1]
    conv = jnp.where(half, low, swap(high)).reshape(CH * n, W)
    back = jnp.where(half, swap(low), high).reshape(CH * n, W)
    conv = dot(conv.astype(BF16), flip)
    gated_ref[...] = (q[...].astype(F32) * conv).astype(BF16)
    qgrad_ref[...] = (g[...].astype(F32) * conv).astype(BF16)
    kgrad_ref[...] = (back * v[...].astype(F32)).astype(BF16)
    vgrad_ref[...] = (back * k[...].astype(F32)).astype(BF16)

    all_of("seq", me_seq, send1, recv1, 0).wait_send()
    all_of("seq", me_seq, send2, recv2, 2).wait_send()
    all_of("chan", me_chan, send3, recv3, 4).wait_send()
    all_of("chan", me_chan, send3, recv3, 4).wait_recv()
    fgrad_ref[...] = jnp.sum(recv3[...], axis=0)


def write_out(*refs):
    count = (len(refs) - 1) // 2
    sem = refs[-1]
    copies = [
        pltpu.make_async_copy(refs[i], refs[count + i], sem.at[i]) for i in range(count)
    ]
    for copy in copies:
        copy.start()
    for copy in copies:
        copy.wait()


def on_device(n, *args):
    rows = CH * n
    length = W * n
    vmem = pl.BlockSpec(memory_space=pltpu.VMEM)
    hbm = pl.BlockSpec(memory_space=pltpu.HBM)
    slab = jax.ShapeDtypeStruct((rows, W), BF16)
    shapes = (slab, slab, slab, slab, jax.ShapeDtypeStruct((CH, W), F32))
    results = pl.pallas_call(
        functools.partial(kernel, n, 1.0 / math.sqrt(length)),
        out_shape=shapes,
        in_specs=[hbm] * 5,
        out_specs=(vmem,) * 5,
        scratch_shapes=[pltpu.VMEM((rows, W), BF16)] * 4
        + [
            pltpu.VMEM((CH, length), BF16),
            pltpu.SemaphoreType.DMA((5,)),
            pltpu.VMEM((n, 8, W), BF16),
            pltpu.VMEM((n, 8, W), BF16),
            pltpu.VMEM((n, 8, W), BF16),
            pltpu.VMEM((n, 8, W), BF16),
            pltpu.VMEM((n, CH, W), F32),
            pltpu.VMEM((n, CH, W), F32),
            pltpu.SemaphoreType.DMA((6,)),
            pltpu.SemaphoreType.REGULAR,
            pltpu.SemaphoreType.REGULAR,
            pltpu.VMEM((rows, W), F32),
            pltpu.VMEM((rows, W), F32),
            pltpu.VMEM((8 * n, W), F32),
            pltpu.VMEM((CH, 2 * n, W), F32),
            pltpu.VMEM((CH, 2 * n, W), F32),
            pltpu.VMEM((8 * n, W), F32),
            pltpu.VMEM((8 * n, W), F32),
            pltpu.VMEM((4, CH, n + 8, W), F32),
            pltpu.VMEM((CH, 4, 2 * n, W), F32),
        ],
        compiler_params=pltpu.CompilerParams(
            collective_id=0, has_side_effects=True, vmem_limit_bytes=32 << 20
        ),
    )(*(pltpu.with_memory_space_constraint(x, pltpu.HBM) for x in args))
    return pl.pallas_call(
        write_out,
        out_shape=shapes,
        in_specs=[vmem] * 5,
        out_specs=(hbm,) * 5,
        scratch_shapes=[pltpu.SemaphoreType.DMA((5,))],
    )(*(pltpu.with_memory_space_constraint(x, pltpu.VMEM) for x in results))


def solution(mesh):
    return jax.shard_map(
        functools.partial(on_device, mesh.shape["seq"]),
        mesh=mesh,
        in_specs=(
            P("chan", "seq"),
            P("chan", "seq"),
            P("chan", "seq"),
            P("chan", "seq"),
            P("seq", None),
        ),
        out_specs=(
            P("chan", "seq"),
            P("chan", "seq"),
            P("chan", "seq"),
            P("chan", "seq"),
            P("seq", "chan"),
        ),
        check_vma=False,
    )
```

```python
import functools
import math

import jax
import jax.numpy as jnp
from jax import lax
from jax.experimental import pallas as pl
from jax.experimental.pallas import tpu as pltpu
from jax.sharding import PartitionSpec as P

MESH = pl.DeviceIdType.MESH
F32 = jnp.float32
BF16 = jnp.bfloat16
W = 128
G = 32
CH = 4


def flip_matrix():
    row = lax.broadcasted_iota(jnp.int32, (W, W), 0)
    col = lax.broadcasted_iota(jnp.int32, (W, W), 1)
    return jnp.where(row + col == W - 1, 1.0, 0.0).astype(BF16)


def dot(left, right):
    return jnp.dot(left, right, preferred_element_type=F32)


def toeplitz_sum(blocks, row_of, left_of):
    row = lax.broadcasted_iota(jnp.int32, (W, W), 0)
    col = lax.broadcasted_iota(jnp.int32, (W, W), 1)
    lower = row >= col
    before = jnp.zeros((W, W), F32)
    total = None
    for k in range(0, blocks, 2):
        parts = []
        for b in (k, k + 1):
            turned = pltpu.roll(
                jnp.broadcast_to(row_of(b), (W, W)), 1, 1, stride=1, stride_axis=0
            )
            parts.append(jnp.where(lower, turned, before).astype(BF16))
            before = turned
        left = jnp.concatenate([left_of(k), left_of(k + 1)], axis=1)
        term = dot(left, jnp.concatenate(parts, axis=0))
        total = term if total is None else total + term
    return total


def shifted_rows(rows_of, turned):
    lane = lax.broadcasted_iota(jnp.int32, (rows_of, W), 1)
    return [
        jnp.where(
            lane < 2 * G,
            jnp.where(lane < G, turned(-r % 4, 0), turned((1 - r) % 4, 1)),
            jnp.where(lane < 3 * G, turned((2 - r) % 4, 2), turned((3 - r) % 4, 3)),
        )
        for r in range(4)
    ]


def lag_sum(blocks, row_of, left_of):
    row = lax.broadcasted_iota(jnp.int32, (G, W), 0)
    col = lax.broadcasted_iota(jnp.int32, (G, W), 1)
    lower = row >= col
    before = jnp.zeros((G, W), F32)
    bases = []
    for k in range(blocks + 1):
        if k < blocks:
            turned = pltpu.roll(
                jnp.broadcast_to(row_of(k), (G, W)), 1, 1, stride=1, stride_axis=0
            )
        else:
            turned = jnp.zeros((G, W), F32)
        bases.append(jnp.where(lower, turned, before).astype(BF16))
        before = turned
    total = None
    step = min(blocks, 8)
    for k in range(0, blocks, step):
        right = jnp.concatenate(
            [jnp.concatenate([bases[b + 1], bases[b]], axis=1) for b in range(k, k + step)], axis=0
        )
        left = jnp.concatenate([left_of(t) for t in range(k // 4, (k + step) // 4)], axis=1)
        term = dot(left, right)
        total = term if total is None else total + term
    lane = lax.broadcasted_iota(jnp.int32, (blocks, W), 1)
    out = total[:blocks, W:]
    for r in range(1, 4):
        part = total[r * blocks : (r + 1) * blocks]
        chosen = jnp.where(lane < W - G * r, part[:, W:], part[:, :W])
        out = out + pltpu.roll(chosen, G * r, 1)
    return out


def kernel(
    n, scale,
    q_hbm, k_hbm, v_hbm, g_hbm, taps_hbm,
    gated_ref, qgrad_ref, kgrad_ref, vgrad_ref, fgrad_ref,
    q, k, v, g, taps, in_sem,
    send1, recv1, send2, recv2, send3, recv3, sems, all_seq, all_chan,
    tap_rows, tap_flip, wide1, pad_p, pad_x, wide2, wide3, turned_p, pad_q,
):
    me_seq = lax.axis_index("seq")
    me_chan = lax.axis_index("chan")
    core = 1 - lax.rem(me_seq, 2)
    pair = me_seq - 1 + 2 * core
    lags_turn = jnp.where(me_chan >= 3 * n // 8, 0, 1)

    loads = [
        pltpu.make_async_copy(src, dst, in_sem.at[i])
        for i, (src, dst) in enumerate(
            ((k_hbm, k), (v_hbm, v), (g_hbm, g), (q_hbm, q), (taps_hbm, taps))
        )
    ]
    for load in loads[:4]:
        load.start()

    barrier = pltpu.get_barrier_semaphore()

    def tell(sem, **to):
        pl.semaphore_signal(sem, inc=1, device_id=to, device_id_type=MESH)

    chips = n // 2
    outer = min(chips, 4)
    inner = chips // outer
    own = (inner // 2) * outer + outer // 2
    my_outer, my_inner = me_seq // (2 * inner), lax.rem(me_seq // 2, inner)

    def chip_at(i):
        at_outer = lax.rem(my_outer + outer // 2 + lax.rem(i, outer), outer)
        at_inner = lax.rem(my_inner + inner // 2 + i // outer, inner)
        return 2 * (at_outer * inner + at_inner)

    def each_other_chip(step):
        def body(i, carry):
            step(chip_at(i))
            return carry

        lax.fori_loop(0, own, body, 0)
        lax.fori_loop(own + 1, chips, body, 0)

    each_other_chip(lambda to: tell(barrier, seq=to + 1))

    @pl.when(core == 1)
    def _():
        tell(barrier, seq=pair)

    loads[4].start()

    def greet_chan(i, carry):
        @pl.when(i != me_chan)
        def _():
            tell(barrier, seq=me_seq - 1 + core, chan=i)

        return carry

    lax.fori_loop(n // 2, 3 * n // 4, greet_chan, 0)
    lax.fori_loop(n // 4, n // 2, greet_chan, 0)

    half = lax.broadcasted_iota(jnp.int32, (CH * n // 8, 8, W), 1) < CH
    flip = flip_matrix()

    def swap(x):
        return pltpu.roll(x, CH, 1)

    for load in loads[:4]:
        load.wait()
    tiles = (CH * n // 8, 8, W)
    mixed = (k[...].astype(F32) * v[...].astype(F32)).astype(BF16)
    mixed = dot(mixed, flip).reshape(tiles)
    pulled = (g[...].astype(F32) * q[...].astype(F32)).reshape(tiles)
    paired = jnp.stack(
        [jnp.where(half, mixed, swap(pulled)), jnp.where(half, swap(mixed), pulled)], axis=1
    )
    send1[...] = paired.reshape(n, 8, W).astype(BF16)

    @pl.when(core == 0)
    def _():
        pl.semaphore_wait(barrier, n - 1)
        tell(all_seq, seq=pair)

    @pl.when(core == 1)
    def _():
        pl.semaphore_wait(all_seq, 1)

    def send_one(axis, me, to, send, recv, at):
        pltpu.make_async_remote_copy(
            src_ref=send.at[to], dst_ref=recv.at[me],
            send_sem=sems.at[at], recv_sem=sems.at[at + 1],
            device_id={axis: to}, device_id_type=MESH,
        ).start()

    def exchange_seq(send, recv, at):
        def both_cores(to):
            send_one("seq", me_seq, to, send, recv, at)
            send_one("seq", me_seq, to + 1, send, recv, at)

        each_other_chip(both_cores)
        send_one("seq", me_seq, pair, send, recv, at)
        recv[me_seq] = send[me_seq]

    def exchange_chan(send, recv, at):
        def step(i, carry):
            send_one("chan", me_chan, i, send, recv, at)
            return carry

        lax.fori_loop(0, me_chan, step, 0)
        lax.fori_loop(me_chan + 1, n, step, 0)
        recv[me_chan] = send[me_chan]

    def all_of(axis, me, send, recv, at):
        return pltpu.make_async_remote_copy(
            src_ref=send.at[pl.ds(0, n - 1)], dst_ref=recv.at[pl.ds(0, n - 1)],
            send_sem=sems.at[at], recv_sem=sems.at[at + 1],
            device_id={axis: lax.rem(me + 1, n)}, device_id_type=MESH,
        )

    exchange_seq(send1, recv1, 0)
    lax.fori_loop(0, n // 4, greet_chan, 0)
    lax.fori_loop(3 * n // 4, n, greet_chan, 0)

    pad_p[...] = jnp.zeros_like(pad_p)
    pad_x[...] = jnp.zeros_like(pad_x)
    pad_q[...] = jnp.zeros_like(pad_q)
    turned_p[...] = jnp.zeros_like(turned_p)

    loads[4].wait()
    tap_values = taps[...].astype(F32)
    for b in range(n):
        tap_rows[CH * b : CH * (b + 1), :] = tap_values[:, W * b : W * (b + 1)]
    tap_flip[...] = dot(tap_rows[...].astype(BF16), flip)

    all_of("seq", me_seq, send1, recv1, 0).wait_recv()
    wide1[...] = recv1[...].reshape(n * 8, W).astype(F32)
    for c in range(CH):
        pad_p[c, :n, :] = wide1[pl.ds(CH + c, n, stride=8), :]
        pad_x[c, n:, :] = wide1[pl.ds(c, n, stride=8), :]

    def pass_chan_on():
        @pl.when(core == 1)
        def _():
            pl.semaphore_wait(barrier, 2 * (n - 1))
            tell(all_chan, seq=pair)

    def lags():
        pl.when(me_chan >= n // 2)(pass_chan_on)
        for c in range(CH):
            for s in range(4):
                own_rows = pad_p[c, :n, :]
                turned_p[s, c, :n, :] = pltpu.roll(own_rows, G * s, 1) if s else own_rows
        for c in range(CH):
            for r, rows in enumerate(
                shifted_rows(n, lambda s, j: turned_p[s, c, j : j + n, :])
            ):
                pad_q[c, r, :n, :] = rows
            wide3[pl.ds(c, n, stride=8), :] = scale * lag_sum(
                n,
                lambda b: pad_x[c, pl.ds(n + b, 1), :],
                lambda t: jnp.concatenate(
                    [pad_q[c, r, 4 * t : 4 * t + n, :].astype(BF16) for r in range(4)], axis=0
                ),
            )
        pl.when(me_chan < n // 2)(pass_chan_on)
        send3[...] = wide3[...].reshape(n, 8, W)[:, :CH, :]
        @pl.when(core == 0)
        def _():
            pl.semaphore_wait(all_chan, 1)

        exchange_chan(send3, recv3, 4)

    def convolutions():
        for c in range(CH):
            both = scale * toeplitz_sum(
                n,
                lambda b: tap_flip[pl.ds(CH * b + c, 1), :],
                lambda b: jnp.concatenate(
                    [
                        pad_p[c, b : b + n, :].astype(BF16),
                        pad_x[c, n - b : 2 * n - b, :].astype(BF16),
                    ],
                    axis=0,
                ),
            )
            wide2[pl.ds(c, n, stride=8), :] = both[n:]
            wide2[pl.ds(CH + c, n, stride=8), :] = both[:n]
        send2[...] = wide2[...].reshape(n, 8, W).astype(BF16)
        exchange_seq(send2, recv2, 2)

    def turn(i, carry):
        pl.when(i == lags_turn)(lags)
        pl.when(i != lags_turn)(convolutions)
        return carry

    lax.fori_loop(0, 2, turn, 0)

    all_of("seq", me_seq, send2, recv2, 2).wait_recv()
    came = recv2[...].astype(F32).reshape(CH * n // 8, 2, 8, W)
    low, high = came[:, 0], came[:, 1]
    conv = jnp.where(half, low, swap(high)).reshape(CH * n, W)
    back = jnp.where(half, swap(low), high).reshape(CH * n, W)
    conv = dot(conv.astype(BF16), flip)
    gated_ref[...] = (q[...].astype(F32) * conv).astype(BF16)
    qgrad_ref[...] = (g[...].astype(F32) * conv).astype(BF16)
    kgrad_ref[...] = (back * v[...].astype(F32)).astype(BF16)
    vgrad_ref[...] = (back * k[...].astype(F32)).astype(BF16)

    all_of("seq", me_seq, send1, recv1, 0).wait_send()
    all_of("seq", me_seq, send2, recv2, 2).wait_send()
    all_of("chan", me_chan, send3, recv3, 4).wait_send()
    all_of("chan", me_chan, send3, recv3, 4).wait_recv()
    fgrad_ref[...] = jnp.sum(recv3[...], axis=0)


def write_out(*refs):
    count = (len(refs) - 1) // 2
    sem = refs[-1]
    copies = [
        pltpu.make_async_copy(refs[i], refs[count + i], sem.at[i]) for i in range(count)
    ]
    for copy in copies:
        copy.start()
    for copy in copies:
        copy.wait()


def on_device(n, *args):
    rows = CH * n
    length = W * n
    vmem = pl.BlockSpec(memory_space=pltpu.VMEM)
    hbm = pl.BlockSpec(memory_space=pltpu.HBM)
    slab = jax.ShapeDtypeStruct((rows, W), BF16)
    shapes = (slab, slab, slab, slab, jax.ShapeDtypeStruct((CH, W), F32))
    results = pl.pallas_call(
        functools.partial(kernel, n, 1.0 / math.sqrt(length)),
        out_shape=shapes,
        in_specs=[hbm] * 5,
        out_specs=(vmem,) * 5,
        scratch_shapes=[pltpu.VMEM((rows, W), BF16)] * 4
        + [
            pltpu.VMEM((CH, length), BF16),
            pltpu.SemaphoreType.DMA((5,)),
            pltpu.VMEM((n, 8, W), BF16),
            pltpu.VMEM((n, 8, W), BF16),
            pltpu.VMEM((n, 8, W), BF16),
            pltpu.VMEM((n, 8, W), BF16),
            pltpu.VMEM((n, CH, W), F32),
            pltpu.VMEM((n, CH, W), F32),
            pltpu.SemaphoreType.DMA((6,)),
            pltpu.SemaphoreType.REGULAR,
            pltpu.SemaphoreType.REGULAR,
            pltpu.VMEM((rows, W), F32),
            pltpu.VMEM((rows, W), F32),
            pltpu.VMEM((8 * n, W), F32),
            pltpu.VMEM((CH, 2 * n, W), F32),
            pltpu.VMEM((CH, 2 * n, W), F32),
            pltpu.VMEM((8 * n, W), F32),
            pltpu.VMEM((8 * n, W), F32),
            pltpu.VMEM((4, CH, n + 8, W), F32),
            pltpu.VMEM((CH, 4, 2 * n, W), F32),
        ],
        compiler_params=pltpu.CompilerParams(
            collective_id=0, has_side_effects=True, vmem_limit_bytes=32 << 20
        ),
    )(*(pltpu.with_memory_space_constraint(x, pltpu.HBM) for x in args))
    return pl.pallas_call(
        write_out,
        out_shape=shapes,
        in_specs=[vmem] * 5,
        out_specs=(hbm,) * 5,
        scratch_shapes=[pltpu.SemaphoreType.DMA((5,))],
    )(*(pltpu.with_memory_space_constraint(x, pltpu.VMEM) for x in results))


def solution(mesh):
    return jax.shard_map(
        functools.partial(on_device, mesh.shape["seq"]),
        mesh=mesh,
        in_specs=(
            P("chan", "seq"),
            P("chan", "seq"),
            P("chan", "seq"),
            P("chan", "seq"),
            P("seq", None),
        ),
        out_specs=(
            P("chan", "seq"),
            P("chan", "seq"),
            P("chan", "seq"),
            P("chan", "seq"),
            P("seq", "chan"),
        ),
        check_vma=False,
    )
```

```python
import functools
import math

import jax
import jax.numpy as jnp
from jax import lax
from jax.experimental import pallas as pl
from jax.experimental.pallas import tpu as pltpu
from jax.sharding import PartitionSpec as P

MESH = pl.DeviceIdType.MESH
F32 = jnp.float32
BF16 = jnp.bfloat16
W = 128
G = 32
CH = 4


def flip_matrix():
    row = lax.broadcasted_iota(jnp.int32, (W, W), 0)
    col = lax.broadcasted_iota(jnp.int32, (W, W), 1)
    return jnp.where(row + col == W - 1, 1.0, 0.0).astype(BF16)


def dot(left, right):
    return jnp.dot(left, right, preferred_element_type=F32)


def toeplitz_sum(blocks, row_of, left_of):
    row = lax.broadcasted_iota(jnp.int32, (W, W), 0)
    col = lax.broadcasted_iota(jnp.int32, (W, W), 1)
    lower = row >= col
    before = jnp.zeros((W, W), F32)
    total = None
    for k in range(0, blocks, 2):
        parts = []
        for b in (k, k + 1):
            turned = pltpu.roll(
                jnp.broadcast_to(row_of(b), (W, W)), 1, 1, stride=1, stride_axis=0
            )
            parts.append(jnp.where(lower, turned, before).astype(BF16))
            before = turned
        left = jnp.concatenate([left_of(k), left_of(k + 1)], axis=1)
        term = dot(left, jnp.concatenate(parts, axis=0))
        total = term if total is None else total + term
    return total


def shifted_rows(rows_of, turned):
    lane = lax.broadcasted_iota(jnp.int32, (rows_of, W), 1)
    return [
        jnp.where(
            lane < 2 * G,
            jnp.where(lane < G, turned(-r % 4, 0), turned((1 - r) % 4, 1)),
            jnp.where(lane < 3 * G, turned((2 - r) % 4, 2), turned((3 - r) % 4, 3)),
        )
        for r in range(4)
    ]


def lag_sum(blocks, row_of, left_of):
    row = lax.broadcasted_iota(jnp.int32, (G, W), 0)
    col = lax.broadcasted_iota(jnp.int32, (G, W), 1)
    lower = row >= col
    before = jnp.zeros((G, W), F32)
    bases = []
    for k in range(blocks + 1):
        if k < blocks:
            turned = pltpu.roll(
                jnp.broadcast_to(row_of(k), (G, W)), 1, 1, stride=1, stride_axis=0
            )
        else:
            turned = jnp.zeros((G, W), F32)
        bases.append(jnp.where(lower, turned, before).astype(BF16))
        before = turned
    total = None
    step = min(blocks, 8)
    for k in range(0, blocks, step):
        right = jnp.concatenate(
            [jnp.concatenate([bases[b + 1], bases[b]], axis=1) for b in range(k, k + step)], axis=0
        )
        left = jnp.concatenate([left_of(t) for t in range(k // 4, (k + step) // 4)], axis=1)
        term = dot(left, right)
        total = term if total is None else total + term
    lane = lax.broadcasted_iota(jnp.int32, (blocks, W), 1)
    out = total[:blocks, W:]
    for r in range(1, 4):
        part = total[r * blocks : (r + 1) * blocks]
        chosen = jnp.where(lane < W - G * r, part[:, W:], part[:, :W])
        out = out + pltpu.roll(chosen, G * r, 1)
    return out


def kernel(
    n, scale,
    q_hbm, k_hbm, v_hbm, g_hbm, taps_hbm,
    gated_ref, qgrad_ref, kgrad_ref, vgrad_ref, fgrad_ref,
    q, k, v, g, taps, in_sem,
    send1, recv1, send2, recv2, send3, recv3, sems, all_seq, all_chan,
    tap_rows, tap_flip, wide1, pad_p, pad_x, wide2, wide3, turned_p, pad_q,
):
    me_seq = lax.axis_index("seq")
    me_chan = lax.axis_index("chan")
    core = 1 - lax.rem(me_seq, 2)
    pair = me_seq - 1 + 2 * core
    lags_turn = jnp.where(me_chan >= 3 * n // 8, 0, 1)

    loads = [
        pltpu.make_async_copy(src, dst, in_sem.at[i])
        for i, (src, dst) in enumerate(
            ((k_hbm, k), (v_hbm, v), (g_hbm, g), (q_hbm, q), (taps_hbm, taps))
        )
    ]
    for load in loads[:4]:
        load.start()

    barrier = pltpu.get_barrier_semaphore()

    def tell(sem, **to):
        pl.semaphore_signal(sem, inc=1, device_id=to, device_id_type=MESH)

    chips = n // 2
    outer = min(chips, 4)
    inner = chips // outer
    own = (inner // 2) * outer + outer // 2
    my_outer, my_inner = me_seq // (2 * inner), lax.rem(me_seq // 2, inner)

    def chip_at(i):
        at_outer = lax.rem(my_outer + outer // 2 + lax.rem(i, outer), outer)
        at_inner = lax.rem(my_inner + inner // 2 + i // outer, inner)
        return 2 * (at_outer * inner + at_inner)

    def each_other_chip(step):
        def body(i, carry):
            step(chip_at(i))
            return carry

        lax.fori_loop(0, own, body, 0)
        lax.fori_loop(own + 1, chips, body, 0)

    @pl.when(core == 1)
    def _():
        tell(barrier, seq=pair)

    each_other_chip(lambda to: tell(barrier, seq=to + 1))

    loads[4].start()

    def greet_chan(i, carry):
        @pl.when(i != me_chan)
        def _():
            tell(barrier, seq=me_seq - 1 + core, chan=i)

        return carry

    far_side = my_inner == inner // 2

    def greet_others():
        lax.fori_loop(0, n // 4, greet_chan, 0)
        lax.fori_loop(3 * n // 4, n, greet_chan, 0)

    lax.fori_loop(n // 2, 3 * n // 4, greet_chan, 0)
    lax.fori_loop(n // 4, n // 2, greet_chan, 0)

    half = lax.broadcasted_iota(jnp.int32, (CH * n // 8, 8, W), 1) < CH
    flip = flip_matrix()

    def swap(x):
        return pltpu.roll(x, CH, 1)

    for load in loads[:4]:
        load.wait()
    tiles = (CH * n // 8, 8, W)
    mixed = (k[...].astype(F32) * v[...].astype(F32)).astype(BF16)
    mixed = dot(mixed, flip).reshape(tiles)
    pulled = (g[...].astype(F32) * q[...].astype(F32)).reshape(tiles)
    paired = jnp.stack(
        [jnp.where(half, mixed, swap(pulled)), jnp.where(half, swap(mixed), pulled)], axis=1
    )
    send1[...] = paired.reshape(n, 8, W).astype(BF16)

    pl.when(jnp.logical_not(far_side))(greet_others)

    @pl.when(core == 0)
    def _():
        pl.semaphore_wait(barrier, n - 1)
        tell(all_seq, seq=pair)

    @pl.when(core == 1)
    def _():
        pl.semaphore_wait(all_seq, 1)

    def send_one(axis, me, to, send, recv, at):
        pltpu.make_async_remote_copy(
            src_ref=send.at[to], dst_ref=recv.at[me],
            send_sem=sems.at[at], recv_sem=sems.at[at + 1],
            device_id={axis: to}, device_id_type=MESH,
        ).start()

    def exchange_seq(send, recv, at):
        def both_cores(to):
            send_one("seq", me_seq, to, send, recv, at)
            send_one("seq", me_seq, to + 1, send, recv, at)

        each_other_chip(both_cores)
        send_one("seq", me_seq, pair, send, recv, at)
        recv[me_seq] = send[me_seq]

    def exchange_chan(send, recv, at):
        def step(i, carry):
            send_one("chan", me_chan, i, send, recv, at)
            return carry

        lax.fori_loop(0, me_chan, step, 0)
        lax.fori_loop(me_chan + 1, n, step, 0)
        recv[me_chan] = send[me_chan]

    def all_of(axis, me, send, recv, at):
        return pltpu.make_async_remote_copy(
            src_ref=send.at[pl.ds(0, n - 1)], dst_ref=recv.at[pl.ds(0, n - 1)],
            send_sem=sems.at[at], recv_sem=sems.at[at + 1],
            device_id={axis: lax.rem(me + 1, n)}, device_id_type=MESH,
        )

    exchange_seq(send1, recv1, 0)
    pl.when(far_side)(greet_others)

    pad_p[...] = jnp.zeros_like(pad_p)
    pad_x[...] = jnp.zeros_like(pad_x)
    pad_q[...] = jnp.zeros_like(pad_q)
    turned_p[...] = jnp.zeros_like(turned_p)

    loads[4].wait()
    tap_values = taps[...].astype(F32)
    for b in range(n):
        tap_rows[CH * b : CH * (b + 1), :] = tap_values[:, W * b : W * (b + 1)]
    tap_flip[...] = dot(tap_rows[...].astype(BF16), flip)

    all_of("seq", me_seq, send1, recv1, 0).wait_recv()
    wide1[...] = recv1[...].reshape(n * 8, W).astype(F32)
    for c in range(CH):
        pad_p[c, :n, :] = wide1[pl.ds(CH + c, n, stride=8), :]
        pad_x[c, n:, :] = wide1[pl.ds(c, n, stride=8), :]

    def pass_chan_on():
        @pl.when(core == 1)
        def _():
            pl.semaphore_wait(barrier, 2 * (n - 1))
            tell(all_chan, seq=pair)

    def lags():
        pl.when(me_chan >= n // 2)(pass_chan_on)
        for c in range(CH):
            for s in range(4):
                own_rows = pad_p[c, :n, :]
                turned_p[s, c, :n, :] = pltpu.roll(own_rows, G * s, 1) if s else own_rows
        for c in range(CH):
            for r, rows in enumerate(
                shifted_rows(n, lambda s, j: turned_p[s, c, j : j + n, :])
            ):
                pad_q[c, r, :n, :] = rows
            wide3[pl.ds(c, n, stride=8), :] = scale * lag_sum(
                n,
                lambda b: pad_x[c, pl.ds(n + b, 1), :],
                lambda t: jnp.concatenate(
                    [pad_q[c, r, 4 * t : 4 * t + n, :].astype(BF16) for r in range(4)], axis=0
                ),
            )
        pl.when(me_chan < n // 2)(pass_chan_on)
        send3[...] = wide3[...].reshape(n, 8, W)[:, :CH, :]
        @pl.when(core == 0)
        def _():
            pl.semaphore_wait(all_chan, 1)

        exchange_chan(send3, recv3, 4)

    def convolutions():
        for c in range(CH):
            both = scale * toeplitz_sum(
                n,
                lambda b: tap_flip[pl.ds(CH * b + c, 1), :],
                lambda b: jnp.concatenate(
                    [
                        pad_p[c, b : b + n, :].astype(BF16),
                        pad_x[c, n - b : 2 * n - b, :].astype(BF16),
                    ],
                    axis=0,
                ),
            )
            wide2[pl.ds(c, n, stride=8), :] = both[n:]
            wide2[pl.ds(CH + c, n, stride=8), :] = both[:n]
        send2[...] = wide2[...].reshape(n, 8, W).astype(BF16)
        exchange_seq(send2, recv2, 2)

    def turn(i, carry):
        pl.when(i == lags_turn)(lags)
        pl.when(i != lags_turn)(convolutions)
        return carry

    lax.fori_loop(0, 2, turn, 0)

    all_of("seq", me_seq, send2, recv2, 2).wait_recv()
    came = recv2[...].astype(F32).reshape(CH * n // 8, 2, 8, W)
    low, high = came[:, 0], came[:, 1]
    conv = jnp.where(half, low, swap(high)).reshape(CH * n, W)
    back = jnp.where(half, swap(low), high).reshape(CH * n, W)
    conv = dot(conv.astype(BF16), flip)
    gated_ref[...] = (q[...].astype(F32) * conv).astype(BF16)
    qgrad_ref[...] = (g[...].astype(F32) * conv).astype(BF16)
    kgrad_ref[...] = (back * v[...].astype(F32)).astype(BF16)
    vgrad_ref[...] = (back * k[...].astype(F32)).astype(BF16)

    all_of("seq", me_seq, send1, recv1, 0).wait_send()
    all_of("seq", me_seq, send2, recv2, 2).wait_send()
    all_of("chan", me_chan, send3, recv3, 4).wait_send()
    all_of("chan", me_chan, send3, recv3, 4).wait_recv()
    fgrad_ref[...] = jnp.sum(recv3[...], axis=0)


def write_out(*refs):
    count = (len(refs) - 1) // 2
    sem = refs[-1]
    copies = [
        pltpu.make_async_copy(refs[i], refs[count + i], sem.at[i]) for i in range(count)
    ]
    for copy in copies:
        copy.start()
    for copy in copies:
        copy.wait()


def on_device(n, *args):
    rows = CH * n
    length = W * n
    vmem = pl.BlockSpec(memory_space=pltpu.VMEM)
    hbm = pl.BlockSpec(memory_space=pltpu.HBM)
    slab = jax.ShapeDtypeStruct((rows, W), BF16)
    shapes = (slab, slab, slab, slab, jax.ShapeDtypeStruct((CH, W), F32))
    results = pl.pallas_call(
        functools.partial(kernel, n, 1.0 / math.sqrt(length)),
        out_shape=shapes,
        in_specs=[hbm] * 5,
        out_specs=(vmem,) * 5,
        scratch_shapes=[pltpu.VMEM((rows, W), BF16)] * 4
        + [
            pltpu.VMEM((CH, length), BF16),
            pltpu.SemaphoreType.DMA((5,)),
            pltpu.VMEM((n, 8, W), BF16),
            pltpu.VMEM((n, 8, W), BF16),
            pltpu.VMEM((n, 8, W), BF16),
            pltpu.VMEM((n, 8, W), BF16),
            pltpu.VMEM((n, CH, W), F32),
            pltpu.VMEM((n, CH, W), F32),
            pltpu.SemaphoreType.DMA((6,)),
            pltpu.SemaphoreType.REGULAR,
            pltpu.SemaphoreType.REGULAR,
            pltpu.VMEM((rows, W), F32),
            pltpu.VMEM((rows, W), F32),
            pltpu.VMEM((8 * n, W), F32),
            pltpu.VMEM((CH, 2 * n, W), F32),
            pltpu.VMEM((CH, 2 * n, W), F32),
            pltpu.VMEM((8 * n, W), F32),
            pltpu.VMEM((8 * n, W), F32),
            pltpu.VMEM((4, CH, n + 8, W), F32),
            pltpu.VMEM((CH, 4, 2 * n, W), F32),
        ],
        compiler_params=pltpu.CompilerParams(
            collective_id=0, has_side_effects=True, vmem_limit_bytes=32 << 20
        ),
    )(*(pltpu.with_memory_space_constraint(x, pltpu.HBM) for x in args))
    return pl.pallas_call(
        write_out,
        out_shape=shapes,
        in_specs=[vmem] * 5,
        out_specs=(hbm,) * 5,
        scratch_shapes=[pltpu.SemaphoreType.DMA((5,))],
    )(*(pltpu.with_memory_space_constraint(x, pltpu.VMEM) for x in results))


def solution(mesh):
    return jax.shard_map(
        functools.partial(on_device, mesh.shape["seq"]),
        mesh=mesh,
        in_specs=(
            P("chan", "seq"),
            P("chan", "seq"),
            P("chan", "seq"),
            P("chan", "seq"),
            P("seq", None),
        ),
        out_specs=(
            P("chan", "seq"),
            P("chan", "seq"),
            P("chan", "seq"),
            P("chan", "seq"),
            P("seq", "chan"),
        ),
        check_vma=False,
    )
```

```python
import functools
import math

import jax
import jax.numpy as jnp
from jax import lax
from jax.experimental import pallas as pl
from jax.experimental.pallas import tpu as pltpu
from jax.sharding import PartitionSpec as P

MESH = pl.DeviceIdType.MESH
F32 = jnp.float32
BF16 = jnp.bfloat16
W = 128
G = 32
CH = 4


def flip_matrix():
    row = lax.broadcasted_iota(jnp.int32, (W, W), 0)
    col = lax.broadcasted_iota(jnp.int32, (W, W), 1)
    return jnp.where(row + col == W - 1, 1.0, 0.0).astype(BF16)


def dot(left, right):
    return jnp.dot(left, right, preferred_element_type=F32)


def toeplitz_sum(blocks, row_of, left_of):
    row = lax.broadcasted_iota(jnp.int32, (W, W), 0)
    col = lax.broadcasted_iota(jnp.int32, (W, W), 1)
    lower = row >= col
    before = jnp.zeros((W, W), F32)
    total = None
    for k in range(0, blocks, 2):
        parts = []
        for b in (k, k + 1):
            turned = pltpu.roll(
                jnp.broadcast_to(row_of(b), (W, W)), 1, 1, stride=1, stride_axis=0
            )
            parts.append(jnp.where(lower, turned, before).astype(BF16))
            before = turned
        left = jnp.concatenate([left_of(k), left_of(k + 1)], axis=1)
        term = dot(left, jnp.concatenate(parts, axis=0))
        total = term if total is None else total + term
    return total


def shifted_rows(rows_of, turned):
    lane = lax.broadcasted_iota(jnp.int32, (rows_of, W), 1)
    return [
        jnp.where(
            lane < 2 * G,
            jnp.where(lane < G, turned(-r % 4, 0), turned((1 - r) % 4, 1)),
            jnp.where(lane < 3 * G, turned((2 - r) % 4, 2), turned((3 - r) % 4, 3)),
        )
        for r in range(4)
    ]


def lag_sum(blocks, row_of, left_of):
    row = lax.broadcasted_iota(jnp.int32, (G, W), 0)
    col = lax.broadcasted_iota(jnp.int32, (G, W), 1)
    lower = row >= col
    before = jnp.zeros((G, W), F32)
    bases = []
    for k in range(blocks + 1):
        if k < blocks:
            turned = pltpu.roll(
                jnp.broadcast_to(row_of(k), (G, W)), 1, 1, stride=1, stride_axis=0
            )
        else:
            turned = jnp.zeros((G, W), F32)
        bases.append(jnp.where(lower, turned, before).astype(BF16))
        before = turned
    total = None
    step = min(blocks, 8)
    for k in range(0, blocks, step):
        right = jnp.concatenate(
            [jnp.concatenate([bases[b + 1], bases[b]], axis=1) for b in range(k, k + step)], axis=0
        )
        left = jnp.concatenate([left_of(t) for t in range(k // 4, (k + step) // 4)], axis=1)
        term = dot(left, right)
        total = term if total is None else total + term
    lane = lax.broadcasted_iota(jnp.int32, (blocks, W), 1)
    out = total[:blocks, W:]
    for r in range(1, 4):
        part = total[r * blocks : (r + 1) * blocks]
        chosen = jnp.where(lane < W - G * r, part[:, W:], part[:, :W])
        out = out + pltpu.roll(chosen, G * r, 1)
    return out


def kernel(
    n, scale,
    q_hbm, k_hbm, v_hbm, g_hbm, taps_hbm,
    gated_ref, qgrad_ref, kgrad_ref, vgrad_ref, fgrad_ref,
    q, k, v, g, taps, in_sem,
    send1, recv1, send2, recv2, send3, recv3, sems, all_seq, all_chan,
    tap_rows, tap_flip, wide1, pad_p, pad_x, wide2, wide3, turned_p, pad_q,
):
    me_seq = lax.axis_index("seq")
    me_chan = lax.axis_index("chan")
    core = 1 - lax.rem(me_seq, 2)
    pair = me_seq - 1 + 2 * core
    lags_turn = jnp.where(me_chan >= 3 * n // 8, 0, 1)

    loads = [
        pltpu.make_async_copy(src, dst, in_sem.at[i])
        for i, (src, dst) in enumerate(
            ((k_hbm, k), (v_hbm, v), (g_hbm, g), (q_hbm, q), (taps_hbm, taps))
        )
    ]
    for load in loads[:4]:
        load.start()

    barrier = pltpu.get_barrier_semaphore()

    def tell(sem, **to):
        pl.semaphore_signal(sem, inc=1, device_id=to, device_id_type=MESH)

    chips = n // 2
    outer = min(chips, 4)
    inner = chips // outer
    own = (inner // 2) * outer + outer // 2
    my_outer, my_inner = me_seq // (2 * inner), lax.rem(me_seq // 2, inner)

    def chip_at(i):
        at_outer = lax.rem(my_outer + outer // 2 + lax.rem(i, outer), outer)
        at_inner = lax.rem(my_inner + inner // 2 + i // outer, inner)
        return 2 * (at_outer * inner + at_inner)

    def each_other_chip(step):
        def body(i, carry):
            step(chip_at(i))
            return carry

        lax.fori_loop(0, own, body, 0, unroll=True)
        lax.fori_loop(own + 1, chips, body, 0, unroll=True)

    @pl.when(core == 1)
    def _():
        tell(barrier, seq=pair)

    each_other_chip(lambda to: tell(barrier, seq=to + 1))

    loads[4].start()

    def greet_chan(i, carry):
        @pl.when(i != me_chan)
        def _():
            tell(barrier, seq=me_seq - 1 + core, chan=i)

        return carry

    far_side = my_inner == inner // 2

    def greet_others():
        lax.fori_loop(0, n // 4, greet_chan, 0, unroll=True)
        lax.fori_loop(3 * n // 4, n, greet_chan, 0, unroll=True)

    lax.fori_loop(n // 2, 3 * n // 4, greet_chan, 0, unroll=True)
    lax.fori_loop(n // 4, n // 2, greet_chan, 0, unroll=True)

    half = lax.broadcasted_iota(jnp.int32, (CH * n // 8, 8, W), 1) < CH
    flip = flip_matrix()

    def swap(x):
        return pltpu.roll(x, CH, 1)

    for load in loads[:4]:
        load.wait()
    tiles = (CH * n // 8, 8, W)
    mixed = (k[...].astype(F32) * v[...].astype(F32)).astype(BF16)
    mixed = dot(mixed, flip).reshape(tiles)
    pulled = (g[...].astype(F32) * q[...].astype(F32)).reshape(tiles)
    paired = jnp.stack(
        [jnp.where(half, mixed, swap(pulled)), jnp.where(half, swap(mixed), pulled)], axis=1
    )
    send1[...] = paired.reshape(n, 8, W).astype(BF16)

    pl.when(jnp.logical_not(far_side))(greet_others)

    @pl.when(core == 0)
    def _():
        pl.semaphore_wait(barrier, n - 1)
        tell(all_seq, seq=pair)

    @pl.when(core == 1)
    def _():
        pl.semaphore_wait(all_seq, 1)

    def send_one(axis, me, to, send, recv, at):
        pltpu.make_async_remote_copy(
            src_ref=send.at[to], dst_ref=recv.at[me],
            send_sem=sems.at[at], recv_sem=sems.at[at + 1],
            device_id={axis: to}, device_id_type=MESH,
        ).start()

    def exchange_seq(send, recv, at):
        def both_cores(to):
            send_one("seq", me_seq, to, send, recv, at)
            send_one("seq", me_seq, to + 1, send, recv, at)

        each_other_chip(both_cores)
        send_one("seq", me_seq, pair, send, recv, at)
        recv[me_seq] = send[me_seq]

    def exchange_chan(send, recv, at):
        def step(i, carry):
            send_one("chan", me_chan, i, send, recv, at)
            return carry

        lax.fori_loop(0, me_chan, step, 0)
        lax.fori_loop(me_chan + 1, n, step, 0)
        recv[me_chan] = send[me_chan]

    def all_of(axis, me, send, recv, at):
        return pltpu.make_async_remote_copy(
            src_ref=send.at[pl.ds(0, n - 1)], dst_ref=recv.at[pl.ds(0, n - 1)],
            send_sem=sems.at[at], recv_sem=sems.at[at + 1],
            device_id={axis: lax.rem(me + 1, n)}, device_id_type=MESH,
        )

    exchange_seq(send1, recv1, 0)
    pl.when(far_side)(greet_others)

    pad_p[...] = jnp.zeros_like(pad_p)
    pad_x[...] = jnp.zeros_like(pad_x)
    pad_q[...] = jnp.zeros_like(pad_q)
    turned_p[...] = jnp.zeros_like(turned_p)

    loads[4].wait()
    tap_values = taps[...].astype(F32)
    for b in range(n):
        tap_rows[CH * b : CH * (b + 1), :] = tap_values[:, W * b : W * (b + 1)]
    tap_flip[...] = dot(tap_rows[...].astype(BF16), flip)

    all_of("seq", me_seq, send1, recv1, 0).wait_recv()
    wide1[...] = recv1[...].reshape(n * 8, W).astype(F32)
    for c in range(CH):
        pad_p[c, :n, :] = wide1[pl.ds(CH + c, n, stride=8), :]
        pad_x[c, n:, :] = wide1[pl.ds(c, n, stride=8), :]

    def pass_chan_on():
        @pl.when(core == 1)
        def _():
            pl.semaphore_wait(barrier, 2 * (n - 1))
            tell(all_chan, seq=pair)

    def lags():
        pl.when(me_chan >= n // 2)(pass_chan_on)
        for c in range(CH):
            for s in range(4):
                own_rows = pad_p[c, :n, :]
                turned_p[s, c, :n, :] = pltpu.roll(own_rows, G * s, 1) if s else own_rows
        for c in range(CH):
            for r, rows in enumerate(
                shifted_rows(n, lambda s, j: turned_p[s, c, j : j + n, :])
            ):
                pad_q[c, r, :n, :] = rows
            wide3[pl.ds(c, n, stride=8), :] = scale * lag_sum(
                n,
                lambda b: pad_x[c, pl.ds(n + b, 1), :],
                lambda t: jnp.concatenate(
                    [pad_q[c, r, 4 * t : 4 * t + n, :].astype(BF16) for r in range(4)], axis=0
                ),
            )
        pl.when(me_chan < n // 2)(pass_chan_on)
        send3[...] = wide3[...].reshape(n, 8, W)[:, :CH, :]
        @pl.when(core == 0)
        def _():
            pl.semaphore_wait(all_chan, 1)

        exchange_chan(send3, recv3, 4)

    def convolutions():
        for c in range(CH):
            both = scale * toeplitz_sum(
                n,
                lambda b: tap_flip[pl.ds(CH * b + c, 1), :],
                lambda b: jnp.concatenate(
                    [
                        pad_p[c, b : b + n, :].astype(BF16),
                        pad_x[c, n - b : 2 * n - b, :].astype(BF16),
                    ],
                    axis=0,
                ),
            )
            wide2[pl.ds(c, n, stride=8), :] = both[n:]
            wide2[pl.ds(CH + c, n, stride=8), :] = both[:n]
        send2[...] = wide2[...].reshape(n, 8, W).astype(BF16)
        exchange_seq(send2, recv2, 2)

    def turn(i, carry):
        pl.when(i == lags_turn)(lags)
        pl.when(i != lags_turn)(convolutions)
        return carry

    lax.fori_loop(0, 2, turn, 0)

    all_of("seq", me_seq, send2, recv2, 2).wait_recv()
    came = recv2[...].astype(F32).reshape(CH * n // 8, 2, 8, W)
    low, high = came[:, 0], came[:, 1]
    conv = jnp.where(half, low, swap(high)).reshape(CH * n, W)
    back = jnp.where(half, swap(low), high).reshape(CH * n, W)
    conv = dot(conv.astype(BF16), flip)
    gated_ref[...] = (q[...].astype(F32) * conv).astype(BF16)
    qgrad_ref[...] = (g[...].astype(F32) * conv).astype(BF16)
    kgrad_ref[...] = (back * v[...].astype(F32)).astype(BF16)
    vgrad_ref[...] = (back * k[...].astype(F32)).astype(BF16)

    all_of("seq", me_seq, send1, recv1, 0).wait_send()
    all_of("seq", me_seq, send2, recv2, 2).wait_send()
    all_of("chan", me_chan, send3, recv3, 4).wait_send()
    all_of("chan", me_chan, send3, recv3, 4).wait_recv()
    fgrad_ref[...] = jnp.sum(recv3[...], axis=0)


def write_out(*refs):
    count = (len(refs) - 1) // 2
    sem = refs[-1]
    copies = [
        pltpu.make_async_copy(refs[i], refs[count + i], sem.at[i]) for i in range(count)
    ]
    for copy in copies:
        copy.start()
    for copy in copies:
        copy.wait()


def on_device(n, *args):
    rows = CH * n
    length = W * n
    vmem = pl.BlockSpec(memory_space=pltpu.VMEM)
    hbm = pl.BlockSpec(memory_space=pltpu.HBM)
    slab = jax.ShapeDtypeStruct((rows, W), BF16)
    shapes = (slab, slab, slab, slab, jax.ShapeDtypeStruct((CH, W), F32))
    results = pl.pallas_call(
        functools.partial(kernel, n, 1.0 / math.sqrt(length)),
        out_shape=shapes,
        in_specs=[hbm] * 5,
        out_specs=(vmem,) * 5,
        scratch_shapes=[pltpu.VMEM((rows, W), BF16)] * 4
        + [
            pltpu.VMEM((CH, length), BF16),
            pltpu.SemaphoreType.DMA((5,)),
            pltpu.VMEM((n, 8, W), BF16),
            pltpu.VMEM((n, 8, W), BF16),
            pltpu.VMEM((n, 8, W), BF16),
            pltpu.VMEM((n, 8, W), BF16),
            pltpu.VMEM((n, CH, W), F32),
            pltpu.VMEM((n, CH, W), F32),
            pltpu.SemaphoreType.DMA((6,)),
            pltpu.SemaphoreType.REGULAR,
            pltpu.SemaphoreType.REGULAR,
            pltpu.VMEM((rows, W), F32),
            pltpu.VMEM((rows, W), F32),
            pltpu.VMEM((8 * n, W), F32),
            pltpu.VMEM((CH, 2 * n, W), F32),
            pltpu.VMEM((CH, 2 * n, W), F32),
            pltpu.VMEM((8 * n, W), F32),
            pltpu.VMEM((8 * n, W), F32),
            pltpu.VMEM((4, CH, n + 8, W), F32),
            pltpu.VMEM((CH, 4, 2 * n, W), F32),
        ],
        compiler_params=pltpu.CompilerParams(
            collective_id=0, has_side_effects=True, vmem_limit_bytes=32 << 20
        ),
    )(*(pltpu.with_memory_space_constraint(x, pltpu.HBM) for x in args))
    return pl.pallas_call(
        write_out,
        out_shape=shapes,
        in_specs=[vmem] * 5,
        out_specs=(hbm,) * 5,
        scratch_shapes=[pltpu.SemaphoreType.DMA((5,))],
    )(*(pltpu.with_memory_space_constraint(x, pltpu.VMEM) for x in results))


def solution(mesh):
    return jax.shard_map(
        functools.partial(on_device, mesh.shape["seq"]),
        mesh=mesh,
        in_specs=(
            P("chan", "seq"),
            P("chan", "seq"),
            P("chan", "seq"),
            P("chan", "seq"),
            P("seq", None),
        ),
        out_specs=(
            P("chan", "seq"),
            P("chan", "seq"),
            P("chan", "seq"),
            P("chan", "seq"),
            P("seq", "chan"),
        ),
        check_vma=False,
    )
```
